32 devices in a mesh: groups: 1, col: 8 (over y, x, core), row: 4 (over z).
Axes of the slice: x: 2, y: 2, z: 4, core: 2. Of those that a mesh axis runs over, the one named last changes fastest.
Arguments:
- features: bfloat16 [16384, 128], P(('groups', 'row', 'col')), may hold values from -6 to 6
- adjacency: bfloat16 [256, 64, 5632], P(('groups', 'col'), None, 'row'), may hold values from -0.125 to 0.125
- tile_cols: int32 [256, 88], P(('groups', 'col'), 'row'), may hold values from 0 to 63
- row_counts: int32 [256, 4], P(('groups', 'col'), 'row'), may hold values from 1 to 22, as said below
- weight: bfloat16 [128, 128], replicated, may hold values from -0.5 to 0.5
- bias: float32 [128], replicated, may hold values from -3 to 3
- out_grad: bfloat16 [16384, 128], P(('groups', 'col', 'row')), may hold values from -6 to 6
Outputs:
- activations: bfloat16 [16384, 128], P(('groups', 'col', 'row'))
- feature_grad: bfloat16 [16384, 128], P(('groups', 'row', 'col'))
- weight_grad: float32 [128, 128], P('groups')
- bias_grad: float32 [128], P('groups')
The draws below stay inside these ranges and needn't reach their ends.
Inputs may be any that keep to these rules, and one draw needn't show every extreme that they name: `row_counts`: live slots of a block row come first among its 22 slots on each row index; at least one entry equals 22. `tile_cols`: block column within the source range of row index s // 22.
All inputs are finite; a program needn't handle non-finite values.
Results may differ from the reference program's by a relative error of at most 0.006.
Values may be sent and summed in bfloat16 or wider, within the bound.
A program may use at most 128 MiB of HBM per device.

```python
import math
import jax
import jax.numpy as jnp
from jax import lax

F = 128
TILE = 64
PER_ROW = 22
NODES = 16384
BLOCKS = 256
ROW_BLKS = 32
COL_BLKS = 64
SLOTS = 88
N_COL = 8
N_ROW = 4


def draw_row_counts(key, part):
    key_cap = jax.random.fold_in(key, 11)
    key_count = jax.random.fold_in(key, 12)
    key_full = jax.random.fold_in(key, 13)
    shape_all = (N_COL, ROW_BLKS, N_ROW)
    caps = jax.random.randint(key_cap, (N_COL, 1, N_ROW), max(PER_ROW // 2, 1), PER_ROW + 1)
    counts = jax.random.randint(key_count, shape_all, 1, caps + 1)
    total = N_COL * ROW_BLKS * N_ROW
    chosen = jax.random.randint(key_full, (), 0, total)
    position = jnp.arange(total, dtype=jnp.int32).reshape(shape_all)
    counts = jnp.where(position == chosen, PER_ROW, counts)
    return counts.reshape(N_COL * ROW_BLKS, N_ROW).astype(jnp.int32)


def place_ends(result, key, least, top_value):
    dims = result.shape
    index_at = [jax.random.randint(jax.random.fold_in(key, axis), (), 0, dims[axis]) for axis in range(len(dims))]
    result = result.at[tuple(index_at)].set(least)
    longest = dims.index(max(dims))
    index_at[longest] = (index_at[longest] + 1) % dims[longest]
    return result.at[tuple(index_at)].set(top_value)


def steps_of(key, extent, cuts, least, top_value):
    loudness, own = 1.0, jax.random.fold_in(key, 6)
    for dim, shards_of in cuts:
        heights = jnp.exp(jax.random.uniform(jax.random.fold_in(own, dim), (shards_of,), jnp.float32, least / len(cuts), top_value / len(cuts)))
        loudness = loudness * jnp.repeat(heights, extent[dim] // shards_of).reshape([-1 if axis == dim else 1 for axis in range(len(extent))])
    return loudness


def normal_values(stream_key, shape, deviation, reach, cuts=(), held_as=jnp.bfloat16):
    result = deviation * jax.random.normal(stream_key, shape, jnp.float32)
    if cuts:
        result = result * steps_of(stream_key, shape, cuts, -0.22, 0.18)
    return jnp.clip(result, -reach, reach).astype(held_as)


def setup_inputs(seed: int = 0, part: int = 0) -> dict:
    arg_keys = jax.random.split(jax.random.key(seed), 8)
    part_keys = jax.random.split(jax.random.fold_in(arg_keys[7], part), 8)
    features = normal_values(part_keys[0], (NODES, F), 1.0, 6.0, ((0, 32),))
    adjacency = normal_values(part_keys[1], (BLOCKS, TILE, SLOTS * TILE), (TILE * SLOTS * 2 // 5) ** -0.5, 0.125, ((0, 8), (2, 4)))
    tile_cols = place_ends(jax.random.randint(part_keys[2], (BLOCKS, SLOTS), 0, COL_BLKS), jax.random.fold_in(part_keys[2], 1), 0, COL_BLKS - 1).astype(jnp.int32)
    row_counts = draw_row_counts(jax.random.fold_in(jax.random.fold_in(arg_keys[7], part), 71), part)
    weight = normal_values(arg_keys[4], (F, F), F ** -0.5, 0.5)
    bias = normal_values(arg_keys[5], (F,), 0.5, 3.0, (), jnp.float32)
    out_grad = normal_values(part_keys[6], (NODES, F), 1.0, 6.0, ((0, 32),))
    return dict(features=features, adjacency=adjacency, tile_cols=tile_cols, row_counts=row_counts, weight=weight, bias=bias, out_grad=out_grad)


def silu_slope(preact):
    sigmoid_z = jax.nn.sigmoid(preact)
    return sigmoid_z * (1.0 + preact * (1.0 - sigmoid_z))

def reference(features, adjacency, tile_cols, row_counts, weight, bias, out_grad):
    group = math.gcd(BLOCKS, 16)
    steps_count = BLOCKS // group
    slot_ids = jnp.arange(SLOTS, dtype=jnp.int32)
    source_block = (tile_cols + (slot_ids // PER_ROW * COL_BLKS)[None, :]).astype(jnp.int32)
    slot_counts = jnp.repeat(row_counts, PER_ROW, axis=1)
    is_live = (slot_ids % PER_ROW)[None, :] < slot_counts
    feature_blocks = features.reshape(BLOCKS, TILE, F)
    tile_groups = adjacency.reshape(steps_count, group, TILE, SLOTS, TILE)
    source_groups = source_block.reshape(steps_count, group, SLOTS)
    live_groups = is_live.reshape(steps_count, group, SLOTS)

    def forward_group(packed):
        tile_part, col_part, live_part = packed
        picked = jnp.where(live_part[:, :, None, None], feature_blocks[col_part], jnp.zeros((), features.dtype))
        return jnp.einsum('bisj,bsjf->bif', tile_part.astype(jnp.float32), picked.astype(jnp.float32))
    summed = lax.map(forward_group, (tile_groups, source_groups, live_groups))
    hidden = summed.reshape(NODES, F).astype(jnp.bfloat16)
    preact = jnp.dot(hidden, weight, preferred_element_type=jnp.float32) + bias
    activations = jax.nn.silu(preact).astype(jnp.bfloat16)
    pre_grad = out_grad.astype(jnp.float32) * silu_slope(preact)
    pre_grad_half = pre_grad.astype(jnp.bfloat16)
    scale = 1.0 / math.sqrt(NODES)
    weight_grad = jnp.dot(hidden.T, pre_grad_half, preferred_element_type=jnp.float32) * scale
    bias_grad = lax.optimization_barrier(jnp.sum(pre_grad, axis=0)) * scale
    dest_grad = jnp.dot(pre_grad_half, weight.T, preferred_element_type=jnp.float32).astype(jnp.bfloat16)
    grad_groups = dest_grad.reshape(steps_count, group, TILE, F)

    def backward_group(accum, packed):
        tile_part, col_part, live_part, grad_part = packed
        contrib = jnp.einsum('bisj,bif->bsjf', tile_part.astype(jnp.float32), grad_part.astype(jnp.float32))
        contrib = jnp.where(live_part[:, :, None, None], contrib, jnp.zeros((), contrib.dtype))
        accum = accum.at[col_part.reshape(-1)].add(contrib.reshape(-1, TILE, F))
        return (accum, None)
    start = jnp.zeros((BLOCKS, TILE, F), jnp.float32)
    accum, unused = lax.scan(backward_group, start, (tile_groups, source_groups, live_groups, grad_groups))
    feature_grad = accum.reshape(NODES, F).astype(jnp.bfloat16)
    return (activations, feature_grad, weight_grad, bias_grad)
```

```python
import functools
import math

import jax
import jax.numpy as jnp
from jax import lax
from jax.experimental import pallas as pl
from jax.experimental.pallas import tpu as pltpu
from jax.sharding import PartitionSpec as P

MESH = pl.DeviceIdType.MESH
F32, BF16 = jnp.float32, jnp.bfloat16
MIB = 1024 * 1024


def col_peers(nc):
    c = lax.axis_index("col")
    outer, core, n_out = c // 2, c % 2, nc // 2
    partner = outer * 2 + (1 - core)
    ahead = [lax.rem(outer + d, n_out) * 2 + core for d in range(n_out)]
    behind = [lax.rem(outer - d + n_out, n_out) * 2 + core for d in range(n_out)]
    return c, partner, ahead, behind


def send(src, dst, send_sem, recv_sem, where):
    return pltpu.make_async_remote_copy(
        src_ref=src, dst_ref=dst, send_sem=send_sem, recv_sem=recv_sem,
        device_id=where, device_id_type=MESH,
    )


def forward_kernel(
    nc, nr, scale, idx_ref, feat_ref, adj_hbm, weight_ref, bias_ref, og_ref,
    act_ref, grads_ref, wb_ref,
    xg, adj, xs, own, part, rbuf, gg,
    a_sem, f_send, f_recv, p_send, p_recv, r_send, r_recv, g_send, g_recv,
):
    blocks, tile, slot_width = adj.shape
    per_row = slot_width // tile
    chunk = blocks // nr
    rows = chunk * tile
    n_out = nc // 2
    own_blocks = feat_ref.shape[0] // tile
    c, partner, ahead, behind = col_peers(nc)
    r = lax.axis_index("row")
    row_at = [lax.rem(r + e, nr) for e in range(nr)]

    loads = []
    for e in range(nr):
        t = row_at[(e + 1) % nr]
        cut = pl.ds(t * chunk, chunk)
        load = pltpu.make_async_copy(adj_hbm.at[cut], adj.at[cut], a_sem.at[e])
        load.start()
        loads.append(load)

    barrier = pltpu.get_barrier_semaphore()
    pl.semaphore_signal(barrier, inc=1, device_id={"col": partner}, device_id_type=MESH)
    for d in range(1, n_out):
        pl.semaphore_signal(barrier, inc=1, device_id={"col": ahead[d]}, device_id_type=MESH)
    for e in range(1, nr):
        pl.semaphore_signal(barrier, inc=1, device_id={"row": row_at[e]}, device_id_type=MESH)

    def blocks_of(col):
        return xg.at[pl.ds(col * own_blocks, own_blocks)]

    xg[pl.ds(c * own_blocks, own_blocks)] = feat_ref[...].reshape(own_blocks, tile, -1)
    xg[nc * own_blocks] = jnp.zeros(xg.shape[1:], xg.dtype)
    pl.semaphore_wait(barrier, 1 + (n_out - 1) + (nr - 1))

    copies = []
    for d in range(1, n_out):
        copy = send(blocks_of(c), blocks_of(c), f_send.at[d], f_recv.at[d], {"col": ahead[d]})
        copy.start()
        copies.append(copy)
    pair = []
    copy = send(blocks_of(c), blocks_of(c), p_send.at[0], p_recv.at[0], {"col": partner})
    copy.start()
    pair.append(copy)
    for d in range(1, n_out):
        copies[d - 1].wait_recv()
        came = blocks_of(behind[d])
        copy = send(came, came, p_send.at[d], p_recv.at[d], {"col": partner})
        copy.start()
        pair.append(copy)
    for copy in pair:
        copy.wait_recv()
    for copy in copies + pair:
        copy.wait_send()

    row_copies = []
    for e in range(nr):
        far = (e + 1) % nr
        t = row_at[far]
        loads[e].wait()

        def block_row(i, carry, t=t, far=far):
            b = t * chunk + i
            for s in range(per_row):
                xs[pl.ds(s * tile, tile)] = xg[idx_ref[b * per_row + s]]
            got = jnp.dot(adj[b], xs[...], preferred_element_type=F32)
            cut = pl.ds(pl.multiple_of(i * tile, tile), tile)
            if far:
                part[far - 1, cut, :] = got.astype(BF16)
            else:
                own[cut, :] = got
            return carry

        lax.fori_loop(0, chunk, block_row, 0)
        if far:
            copy = send(
                part.at[far - 1], rbuf.at[far - 1], r_send.at[far - 1], r_recv.at[far - 1], {"row": t}
            )
            copy.start()
            row_copies.append(copy)
    summed = own[...]
    for copy in row_copies:
        copy.wait_recv()
    for e in range(nr - 1):
        summed = summed + rbuf[e].astype(F32)
    hidden = summed.astype(BF16)
    preact = jnp.dot(hidden, weight_ref[...], preferred_element_type=F32) + bias_ref[...]
    sig = jax.nn.sigmoid(preact)
    pre_grad = og_ref[...].astype(F32) * (sig * (1.0 + preact * (1.0 - sig)))
    half = pre_grad.astype(BF16)
    dest = lax.dot_general(
        half, weight_ref[...], (((1,), (1,)), ((), ())), preferred_element_type=F32
    )
    gg[r] = dest.astype(BF16)
    grad_copies = []
    for e in range(1, nr):
        copy = send(gg.at[r], gg.at[r], g_send.at[e - 1], g_recv.at[e - 1], {"row": row_at[e]})
        copy.start()
        grad_copies.append(copy)
    act_ref[...] = (preact * sig).astype(BF16)
    wb_ref[pl.ds(0, hidden.shape[1]), :] = scale * lax.dot_general(
        hidden, half, (((0,), (0,)), ((), ())), preferred_element_type=F32
    )
    wb_ref[pl.ds(hidden.shape[1], 8), :] = jnp.broadcast_to(
        scale * jnp.sum(pre_grad, axis=0, keepdims=True), (8, hidden.shape[1])
    )
    for copy in grad_copies:
        copy.wait_recv()
    grads_ref[...] = gg[...].reshape(grads_ref.shape)
    for copy in row_copies + grad_copies:
        copy.wait_send()


def backward_kernel(group, idx_ref, adj_ref, grad_ref, out_ref, *accs):
    step = pl.program_id(0)
    unused, tile, slot_width = adj_ref.shape
    per_row = slot_width // tile

    @pl.when(step == 0)
    def start():
        for acc in accs:
            acc[...] = jnp.zeros_like(acc)

    def block_row(i, carry):
        b = step * group + i
        contrib = lax.dot_general(
            adj_ref[i], grad_ref[pl.ds(pl.multiple_of(i * tile, tile), tile), :],
            (((0,), (0,)), ((), ())), preferred_element_type=F32,
        )
        for s in range(per_row):
            acc = accs[s % len(accs)]
            j = idx_ref[b * per_row + s]
            acc[j] = acc[j] + contrib[s * tile : (s + 1) * tile]
        return carry

    lax.fori_loop(0, group, block_row, 0)

    @pl.when(step == pl.num_programs(0) - 1)
    def finish():
        n = out_ref.shape[0]
        total = accs[0][pl.ds(0, n)]
        for acc in accs[1:]:
            total = total + acc[pl.ds(0, n)]
        out_ref[...] = total.astype(BF16)


def scatter_kernel(nc, part_ref, out_ref, from_pair, send_buf, from_chip, p_send, p_recv, s_send, s_recv):
    n_out = nc // 2
    c, partner, ahead, behind = col_peers(nc)
    partner_ahead = [x + partner - c for x in ahead]
    barrier = pltpu.get_barrier_semaphore()
    pl.semaphore_signal(barrier, inc=1, device_id={"col": partner}, device_id_type=MESH)
    for d in range(1, n_out):
        pl.semaphore_signal(barrier, inc=1, device_id={"col": ahead[d]}, device_id_type=MESH)
    pl.semaphore_wait(barrier, n_out)
    order = list(range(1, n_out)) + [0]
    pair = {}
    for d in order:
        pair[d] = send(
            part_ref.at[partner_ahead[d]], from_pair.at[d], p_send.at[d], p_recv.at[d], {"col": partner}
        )
        pair[d].start()
    copies = []
    for d in order:
        pair[d].wait_recv()
        both = part_ref[ahead[d]].astype(F32) + from_pair[d].astype(F32)
        if d:
            send_buf[d - 1] = both.astype(BF16)
            copy = send(
                send_buf.at[d - 1], from_chip.at[d - 1], s_send.at[d - 1], s_recv.at[d - 1], {"col": ahead[d]}
            )
            copy.start()
            copies.append(copy)
    for d in range(1, n_out):
        copies[d - 1].wait_recv()
        both = both + from_chip[d - 1].astype(F32)
    out_ref[...] = both.astype(BF16)
    for copy in copies + [pair[d] for d in order]:
        copy.wait_send()


def on_device(mesh, features, adjacency, tile_cols, row_counts, weight, bias, out_grad):
    blocks, tile, slot_width = adjacency.shape
    per_row = slot_width // tile
    own_rows, feat = features.shape
    nc, nr = mesh.shape["col"], mesh.shape["row"]
    n_out = nc // 2
    col_blocks = nc * own_rows // tile
    scale = 1.0 / math.sqrt(own_rows * nc * nr)
    live = jnp.arange(per_row, dtype=jnp.int32)[None, :] < row_counts
    idx = jnp.where(live, tile_cols, col_blocks).reshape(-1)

    vmem = pl.BlockSpec(memory_space=pltpu.VMEM)
    smem = pl.BlockSpec(memory_space=pltpu.SMEM)
    hbm = pl.BlockSpec(memory_space=pl.ANY)
    dma = pltpu.SemaphoreType.DMA
    rows = blocks * tile // nr
    tile_flops = 2 * blocks * tile * slot_width * feat
    activations, grads, wb = pl.pallas_call(
        functools.partial(forward_kernel, nc, nr, scale),
        out_shape=(
            jax.ShapeDtypeStruct((rows, feat), BF16),
            jax.ShapeDtypeStruct((blocks * tile, feat), BF16),
            jax.ShapeDtypeStruct((feat + 8, feat), F32),
        ),
        in_specs=[smem, vmem, hbm, vmem, vmem, vmem],
        out_specs=(vmem, vmem, vmem),
        scratch_shapes=[
            pltpu.VMEM((col_blocks + 1, tile, feat), BF16),
            pltpu.VMEM((blocks, tile, slot_width), BF16),
            pltpu.VMEM((slot_width, feat), BF16),
            pltpu.VMEM((rows, feat), F32),
            pltpu.VMEM((nr - 1, rows, feat), BF16),
            pltpu.VMEM((nr - 1, rows, feat), BF16),
            pltpu.VMEM((nr, rows, feat), BF16),
            dma((nr,)), dma((n_out,)), dma((n_out,)), dma((n_out,)), dma((n_out,)),
            dma((nr - 1,)), dma((nr - 1,)), dma((nr - 1,)), dma((nr - 1,)),
        ],
        compiler_params=pltpu.CompilerParams(
            collective_id=0, has_side_effects=True, vmem_limit_bytes=40 * MIB
        ),
        cost_estimate=pl.CostEstimate(
            flops=tile_flops, bytes_accessed=adjacency.size * 2, transcendentals=rows * feat
        ),
    )(idx, features, adjacency, weight, bias.reshape(1, -1), out_grad)

    wb = lax.psum(wb, ("col", "row"))

    group = math.gcd(blocks, 4)
    partial = pl.pallas_call(
        functools.partial(backward_kernel, group),
        grid=(blocks // group,),
        out_shape=jax.ShapeDtypeStruct((col_blocks, tile, feat), BF16),
        in_specs=[
            smem,
            pl.BlockSpec((group, tile, slot_width), lambda i: (i, 0, 0)),
            pl.BlockSpec((group * tile, feat), lambda i: (i, 0)),
        ],
        out_specs=pl.BlockSpec((col_blocks, tile, feat), lambda i: (0, 0, 0)),
        scratch_shapes=[pltpu.VMEM((col_blocks + 1, tile, feat), F32) for unused in range(2)],
        compiler_params=pltpu.CompilerParams(vmem_limit_bytes=40 * MIB),
        cost_estimate=pl.CostEstimate(
            flops=tile_flops * 8, bytes_accessed=adjacency.size * 2, transcendentals=0
        ),
    )(idx, adjacency, grads)

    feature_grad = pl.pallas_call(
        functools.partial(scatter_kernel, nc),
        out_shape=jax.ShapeDtypeStruct((own_rows, feat), BF16),
        in_specs=[vmem],
        out_specs=vmem,
        scratch_shapes=[
            pltpu.VMEM((n_out, own_rows, feat), BF16),
            pltpu.VMEM((n_out - 1, own_rows, feat), BF16),
            pltpu.VMEM((n_out - 1, own_rows, feat), BF16),
            dma((n_out,)), dma((n_out,)), dma((n_out - 1,)), dma((n_out - 1,)),
        ],
        compiler_params=pltpu.CompilerParams(
            collective_id=1, has_side_effects=True, vmem_limit_bytes=20 * MIB
        ),
        cost_estimate=pl.CostEstimate(
            flops=own_rows * nc * feat, bytes_accessed=8 * own_rows * nc * feat, transcendentals=0
        ),
    )(partial.reshape(nc, own_rows, feat))
    return (activations, feature_grad, wb[:feat], wb[feat])


def solution(mesh):
    placed = (
        P(("groups", "row", "col"), None),
        P(("groups", "col"), None, "row"),
        P(("groups", "col"), "row"),
        P(("groups", "col"), "row"),
        P(),
        P(),
        P(("groups", "col", "row"), None),
    )
    return jax.shard_map(
        functools.partial(on_device, mesh),
        mesh=mesh,
        in_specs=placed,
        out_specs=(
            P(("groups", "col", "row"), None),
            P(("groups", "row", "col"), None),
            P("groups", None),
            P("groups"),
        ),
        check_vma=False,
    )
```

```python
import functools
import math

import jax
import jax.numpy as jnp
from jax import lax
from jax.experimental import pallas as pl
from jax.experimental.pallas import tpu as pltpu
from jax.sharding import PartitionSpec as P

MESH = pl.DeviceIdType.MESH
F32, BF16 = jnp.float32, jnp.bfloat16
MIB = 1024 * 1024


def col_peers(nc):
    c = lax.axis_index("col")
    outer, core, n_out = c // 2, c % 2, nc // 2
    partner = outer * 2 + (1 - core)
    ahead = [lax.rem(outer + d, n_out) * 2 + core for d in range(n_out)]
    behind = [lax.rem(outer - d + n_out, n_out) * 2 + core for d in range(n_out)]
    return c, partner, ahead, behind


def send(src, dst, send_sem, recv_sem, where):
    return pltpu.make_async_remote_copy(
        src_ref=src, dst_ref=dst, send_sem=send_sem, recv_sem=recv_sem,
        device_id=where, device_id_type=MESH,
    )


def forward_kernel(
    nc, nr, scale, cols_ref, counts_ref, feat_hbm, adj_hbm, weight_hbm, bias_hbm, og_hbm,
    act_ref, grads_ref, wb_ref,
    xg, adj, weight_ref, bias_ref, og_ref, own, part, rbuf, gg,
    in_sem, a_sem, f_send, f_recv, p_send, p_recv, r_send, r_recv, g_send, g_recv,
):
    blocks, tile, slot_width = adj.shape
    per_row = slot_width // tile
    chunk = blocks // nr
    rows = chunk * tile
    n_out = nc // 2
    own_blocks = feat_hbm.shape[0]
    c, partner, ahead, behind = col_peers(nc)
    r = lax.axis_index("row")
    row_at = [lax.rem(r + e, nr) for e in range(nr)]

    mine = xg.at[pl.ds(c * own_blocks, own_blocks)]
    first = pltpu.make_async_copy(feat_hbm, mine, in_sem.at[0])
    first.start()
    loads = []
    for e in range(nr):
        t = row_at[(e + 1) % nr]
        cut = pl.ds(t * chunk, chunk)
        load = pltpu.make_async_copy(adj_hbm.at[cut], adj.at[cut], a_sem.at[e])
        load.start()
        loads.append(load)
    small = []
    for n, (src, dst) in enumerate(((weight_hbm, weight_ref), (bias_hbm, bias_ref), (og_hbm, og_ref))):
        load = pltpu.make_async_copy(src, dst, in_sem.at[n + 1])
        load.start()
        small.append(load)

    barrier = pltpu.get_barrier_semaphore()
    pl.semaphore_signal(barrier, inc=1, device_id={"col": partner}, device_id_type=MESH)
    for d in range(1, n_out):
        pl.semaphore_signal(barrier, inc=1, device_id={"col": ahead[d]}, device_id_type=MESH)
    for e in range(1, nr):
        pl.semaphore_signal(barrier, inc=1, device_id={"row": row_at[e]}, device_id_type=MESH)

    def blocks_of(col):
        return xg.at[pl.ds(col * own_blocks, own_blocks)]

    xg[nc * own_blocks] = jnp.zeros(xg.shape[1:], xg.dtype)
    first.wait()
    pl.semaphore_wait(barrier, 1 + (n_out - 1) + (nr - 1))

    copies = []
    for d in range(1, n_out):
        copy = send(blocks_of(c), blocks_of(c), f_send.at[d], f_recv.at[d], {"col": ahead[d]})
        copy.start()
        copies.append(copy)
    pair = []
    copy = send(blocks_of(c), blocks_of(c), p_send.at[0], p_recv.at[0], {"col": partner})
    copy.start()
    pair.append(copy)
    for d in range(1, n_out):
        copies[d - 1].wait_recv()
        came = blocks_of(behind[d])
        copy = send(came, came, p_send.at[d], p_recv.at[d], {"col": partner})
        copy.start()
        pair.append(copy)
    for copy in pair:
        copy.wait_recv()
    for copy in copies + pair:
        copy.wait_send()

    row_copies = []
    for e in range(nr):
        far = (e + 1) % nr
        t = row_at[far]
        loads[e].wait()

        def block_row(i, carry, t=t, far=far):
            b = t * chunk + i
            count = counts_ref[b, 0]
            picked = [
                xg[jnp.where(s < count, cols_ref[b, s], nc * own_blocks)] for s in range(per_row)
            ]
            got = jnp.dot(adj[b], jnp.concatenate(picked, axis=0), preferred_element_type=F32)
            cut = pl.ds(pl.multiple_of(i * tile, tile), tile)
            if far:
                part[far - 1, cut, :] = got.astype(BF16)
            else:
                own[cut, :] = got
            return carry

        lax.fori_loop(0, chunk, block_row, 0)
        if far:
            copy = send(
                part.at[far - 1], rbuf.at[far - 1], r_send.at[far - 1], r_recv.at[far - 1], {"row": t}
            )
            copy.start()
            row_copies.append(copy)
    summed = own[...]
    for copy in row_copies:
        copy.wait_recv()
    for e in range(nr - 1):
        summed = summed + rbuf[e].astype(F32)
    hidden = summed.astype(BF16)
    for load in small:
        load.wait()
    preact = jnp.dot(hidden, weight_ref[...], preferred_element_type=F32) + bias_ref[...]
    sig = jax.nn.sigmoid(preact)
    pre_grad = og_ref[...].astype(F32) * (sig * (1.0 + preact * (1.0 - sig)))
    half = pre_grad.astype(BF16)
    dest = lax.dot_general(
        half, weight_ref[...], (((1,), (1,)), ((), ())), preferred_element_type=F32
    )
    gg[r] = dest.astype(BF16)
    grad_copies = []
    for e in range(1, nr):
        copy = send(gg.at[r], gg.at[r], g_send.at[e - 1], g_recv.at[e - 1], {"row": row_at[e]})
        copy.start()
        grad_copies.append(copy)
    act_ref[...] = (preact * sig).astype(BF16)
    feat = hidden.shape[1]
    cut = feat // nr
    wb_ref[:, pl.ds(0, cut), :] = scale * lax.dot_general(
        hidden, half, (((0,), (0,)), ((), ())), preferred_element_type=F32
    ).reshape(nr, cut, feat)
    wb_ref[:, pl.ds(cut, 8), :] = jnp.broadcast_to(
        scale * jnp.sum(pre_grad, axis=0, keepdims=True), (nr, 8, feat)
    )
    for copy in grad_copies:
        copy.wait_recv()
    grads_ref[...] = gg[...].reshape(grads_ref.shape)
    for copy in row_copies + grad_copies:
        copy.wait_send()


def backward_kernel(group, cols_ref, counts_ref, adj_hbm, grad_ref, out_ref, adj, a_sem, *accs):
    blocks, tile, slot_width = adj.shape
    per_row = slot_width // tile
    dead = out_ref.shape[0]

    def load(g):
        cut = pl.ds(g * group, group)
        return pltpu.make_async_copy(adj_hbm.at[cut], adj.at[cut], a_sem.at[g])

    for g in range(blocks // group):
        load(g).start()
    for acc in accs:
        acc[...] = jnp.zeros_like(acc)

    def block_row(i, g):
        b = g * group + i
        contrib = lax.dot_general(
            adj[b], grad_ref[pl.ds(pl.multiple_of(b * tile, tile), tile), :],
            (((0,), (0,)), ((), ())), preferred_element_type=F32,
        )
        count = counts_ref[b, 0]
        for s in range(per_row):
            acc = accs[s % len(accs)]
            j = jnp.where(s < count, cols_ref[b, s], dead)
            acc[j] = acc[j] + contrib[s * tile : (s + 1) * tile]
        return g

    def block_rows(g, carry):
        load(g).wait()
        lax.fori_loop(0, group, block_row, g)
        return carry

    lax.fori_loop(0, blocks // group, block_rows, 0)
    total = accs[0][pl.ds(0, dead)]
    for acc in accs[1:]:
        total = total + acc[pl.ds(0, dead)]
    out_ref[...] = total.astype(BF16)


def scatter_kernel(
    nc, nr, part_ref, wb_ref, out_ref, wg_ref, bg_ref,
    from_pair, send_buf, from_chip, w_row, w_sum, w_pair, w_chip, w_all,
    p_send, p_recv, s_send, s_recv, wr_send, wr_recv, wp_send, wp_recv, wc_send, wc_recv, wa_send, wa_recv,
):
    n_out = nc // 2
    c, partner, ahead, behind = col_peers(nc)
    outer = c // 2
    r = lax.axis_index("row")
    row_at = [lax.rem(r + e, nr) for e in range(nr)]
    partner_ahead = [x + partner - c for x in ahead]
    barrier = pltpu.get_barrier_semaphore()
    pl.semaphore_signal(barrier, inc=1, device_id={"col": partner}, device_id_type=MESH)
    for d in range(1, n_out):
        pl.semaphore_signal(barrier, inc=1, device_id={"col": ahead[d]}, device_id_type=MESH)
    for e in range(1, nr):
        pl.semaphore_signal(barrier, inc=1, device_id={"row": row_at[e]}, device_id_type=MESH)
    pl.semaphore_wait(barrier, n_out + nr - 1)

    started = []

    def go(*args):
        copy = send(*args)
        copy.start()
        started.append(copy)
        return copy

    order = list(range(1, n_out)) + [0]
    pair = {}
    for d in order:
        pair[d] = go(part_ref.at[partner_ahead[d]], from_pair.at[d], p_send.at[d], p_recv.at[d], {"col": partner})
    w_copies = [
        go(wb_ref.at[row_at[e]], w_row.at[e - 1], wr_send.at[e - 1], wr_recv.at[e - 1], {"row": row_at[e]})
        for e in range(1, nr)
    ]
    copies = []
    for d in order:
        pair[d].wait_recv()
        both = part_ref[ahead[d]].astype(F32) + from_pair[d].astype(F32)
        if d:
            send_buf[d - 1] = both.astype(BF16)
            copies.append(go(
                send_buf.at[d - 1], from_chip.at[d - 1], s_send.at[d - 1], s_recv.at[d - 1], {"col": ahead[d]}
            ))
    total = wb_ref[r]
    for e in range(1, nr):
        w_copies[e - 1].wait_recv()
        total = total + w_row[e - 1]
    w_sum[...] = total
    go(w_sum, w_pair, wp_send.at[0], wp_recv.at[0], {"col": partner}).wait_recv()
    w_chip[outer] = w_sum[...] + w_pair[...]
    w_copies = [
        go(w_chip.at[outer], w_chip.at[outer], wc_send.at[d - 1], wc_recv.at[d - 1], {"col": ahead[d]})
        for d in range(1, n_out)
    ]
    for copy in w_copies:
        copy.wait_recv()
    total = w_chip[0]
    for n in range(1, n_out):
        total = total + w_chip[n]
    w_all[r] = total
    w_copies = [
        go(w_all.at[r], w_all.at[r], wa_send.at[e - 1], wa_recv.at[e - 1], {"row": row_at[e]})
        for e in range(1, nr)
    ]
    for copy in copies:
        copy.wait_recv()
    for d in range(1, n_out):
        both = both + from_chip[d - 1].astype(F32)
    out_ref[...] = both.astype(BF16)
    for copy in w_copies:
        copy.wait_recv()
    cut = wg_ref.shape[0] // nr
    for n in range(nr):
        wg_ref[pl.ds(n * cut, cut), :] = w_all[n, pl.ds(0, cut), :]
    bg_ref[...] = w_all[0, pl.ds(cut, 1), :]
    for copy in started:
        copy.wait_send()


def on_device(mesh, features, adjacency, tile_cols, row_counts, weight, bias, out_grad):
    blocks, tile, slot_width = adjacency.shape
    own_rows, feat = features.shape
    nc, nr = mesh.shape["col"], mesh.shape["row"]
    n_out = nc // 2
    col_blocks = nc * own_rows // tile
    scale = 1.0 / math.sqrt(own_rows * nc * nr)
    cut = feat // nr

    vmem = pl.BlockSpec(memory_space=pltpu.VMEM)
    smem = pl.BlockSpec(memory_space=pltpu.SMEM)
    hbm = pl.BlockSpec(memory_space=pltpu.HBM)
    dma = pltpu.SemaphoreType.DMA
    rows = blocks * tile // nr
    tile_flops = 2 * blocks * tile * slot_width * feat
    activations, grads, wb = pl.pallas_call(
        functools.partial(forward_kernel, nc, nr, scale),
        out_shape=(
            jax.ShapeDtypeStruct((rows, feat), BF16),
            jax.ShapeDtypeStruct((blocks * tile, feat), BF16),
            jax.ShapeDtypeStruct((nr, cut + 8, feat), F32),
        ),
        in_specs=[smem, smem, hbm, hbm, hbm, hbm, hbm],
        out_specs=(vmem, vmem, vmem),
        scratch_shapes=[
            pltpu.VMEM((col_blocks + 1, tile, feat), BF16),
            pltpu.VMEM((blocks, tile, slot_width), BF16),
            pltpu.VMEM((feat, feat), BF16),
            pltpu.VMEM((1, feat), F32),
            pltpu.VMEM((rows, feat), BF16),
            pltpu.VMEM((rows, feat), F32),
            pltpu.VMEM((nr - 1, rows, feat), BF16),
            pltpu.VMEM((nr - 1, rows, feat), BF16),
            pltpu.VMEM((nr, rows, feat), BF16),
            dma((4,)), dma((nr,)), dma((n_out,)), dma((n_out,)), dma((n_out,)), dma((n_out,)),
            dma((nr - 1,)), dma((nr - 1,)), dma((nr - 1,)), dma((nr - 1,)),
        ],
        compiler_params=pltpu.CompilerParams(
            collective_id=0, has_side_effects=True, vmem_limit_bytes=60 * MIB
        ),
        cost_estimate=pl.CostEstimate(
            flops=tile_flops, bytes_accessed=adjacency.size * 2, transcendentals=rows * feat
        ),
    )(
        tile_cols, row_counts, features.reshape(own_rows // tile, tile, feat), adjacency, weight,
        bias.reshape(1, -1), out_grad,
    )

    group = math.gcd(blocks, 4)
    partial = pl.pallas_call(
        functools.partial(backward_kernel, group),
        out_shape=jax.ShapeDtypeStruct((col_blocks, tile, feat), BF16),
        in_specs=[smem, smem, hbm, vmem],
        out_specs=vmem,
        scratch_shapes=[
            pltpu.VMEM((blocks, tile, slot_width), BF16),
            dma((blocks // group,)),
        ] + [pltpu.VMEM((col_blocks + 1, tile, feat), F32) for unused in range(2)],
        compiler_params=pltpu.CompilerParams(vmem_limit_bytes=60 * MIB),
        cost_estimate=pl.CostEstimate(
            flops=tile_flops * 8, bytes_accessed=adjacency.size * 2, transcendentals=0
        ),
    )(tile_cols, row_counts, adjacency, grads)

    feature_grad, weight_grad, bias_grad = pl.pallas_call(
        functools.partial(scatter_kernel, nc, nr),
        out_shape=(
            jax.ShapeDtypeStruct((own_rows, feat), BF16),
            jax.ShapeDtypeStruct((feat, feat), F32),
            jax.ShapeDtypeStruct((1, feat), F32),
        ),
        in_specs=[vmem, vmem],
        out_specs=(vmem, vmem, vmem),
        scratch_shapes=[
            pltpu.VMEM((n_out, own_rows, feat), BF16),
            pltpu.VMEM((n_out - 1, own_rows, feat), BF16),
            pltpu.VMEM((n_out - 1, own_rows, feat), BF16),
            pltpu.VMEM((nr - 1, cut + 8, feat), F32),
            pltpu.VMEM((cut + 8, feat), F32),
            pltpu.VMEM((cut + 8, feat), F32),
            pltpu.VMEM((n_out, cut + 8, feat), F32),
            pltpu.VMEM((nr, cut + 8, feat), F32),
            dma((n_out,)), dma((n_out,)), dma((n_out - 1,)), dma((n_out - 1,)),
            dma((nr - 1,)), dma((nr - 1,)), dma((1,)), dma((1,)),
            dma((n_out - 1,)), dma((n_out - 1,)), dma((nr - 1,)), dma((nr - 1,)),
        ],
        compiler_params=pltpu.CompilerParams(
            collective_id=1, has_side_effects=True, vmem_limit_bytes=20 * MIB
        ),
        cost_estimate=pl.CostEstimate(
            flops=own_rows * nc * feat, bytes_accessed=8 * own_rows * nc * feat, transcendentals=0
        ),
    )(partial.reshape(nc, own_rows, feat), wb)
    return (activations, feature_grad, weight_grad, bias_grad.reshape(-1))


def solution(mesh):
    placed = (
        P(("groups", "row", "col"), None),
        P(("groups", "col"), None, "row"),
        P(("groups", "col"), "row"),
        P(("groups", "col"), "row"),
        P(),
        P(),
        P(("groups", "col", "row"), None),
    )
    return jax.shard_map(
        functools.partial(on_device, mesh),
        mesh=mesh,
        in_specs=placed,
        out_specs=(
            P(("groups", "col", "row"), None),
            P(("groups", "row", "col"), None),
            P("groups", None),
            P("groups"),
        ),
        check_vma=False,
    )
```

```python
import functools
import math

import jax
import jax.numpy as jnp
from jax import lax
from jax.experimental import pallas as pl
from jax.experimental.pallas import tpu as pltpu
from jax.sharding import PartitionSpec as P

MESH = pl.DeviceIdType.MESH
F32, BF16 = jnp.float32, jnp.bfloat16
MIB = 1024 * 1024


def col_peers(nc):
    c = lax.axis_index("col")
    outer, core, n_out = c // 2, c % 2, nc // 2
    partner = outer * 2 + (1 - core)
    ahead = [lax.rem(outer + d, n_out) * 2 + core for d in range(n_out)]
    behind = [lax.rem(outer - d + n_out, n_out) * 2 + core for d in range(n_out)]
    return c, partner, ahead, behind


def send(src, dst, send_sem, recv_sem, where):
    return pltpu.make_async_remote_copy(
        src_ref=src, dst_ref=dst, send_sem=send_sem, recv_sem=recv_sem,
        device_id=where, device_id_type=MESH,
    )


def enter(nc, nr):
    c, r = lax.axis_index("col"), lax.axis_index("row")
    barrier = pltpu.get_barrier_semaphore()
    for d in range(1, nc):
        pl.semaphore_signal(barrier, inc=1, device_id={"col": lax.rem(c + d, nc)}, device_id_type=MESH)
    for e in range(1, nr):
        pl.semaphore_signal(barrier, inc=1, device_id={"row": lax.rem(r + e, nr)}, device_id_type=MESH)
    pl.semaphore_wait(barrier, nc - 1 + nr - 1)


def forward_kernel(
    nc, nr, scale, cols_ref, counts_ref, feat_hbm, adj_hbm, weight_hbm, bias_hbm, og_hbm,
    act_ref, grads_ref, wb_ref,
    xg, adj, weight_ref, bias_ref, og_ref, own, part, rbuf, gg, w_out, w_in,
    in_sem, a_sem, f_send, f_recv, p_send, p_recv, r_send, r_recv, g_send, g_recv, w_send, w_recv,
):
    blocks, tile, slot_width = adj.shape
    per_row = slot_width // tile
    chunk = blocks // nr
    rows = chunk * tile
    n_out = nc // 2
    own_blocks = feat_hbm.shape[0]
    c, partner, ahead, behind = col_peers(nc)
    r = lax.axis_index("row")
    row_at = [lax.rem(r + e, nr) for e in range(nr)]

    mine = xg.at[pl.ds(c * own_blocks, own_blocks)]
    first = pltpu.make_async_copy(feat_hbm, mine, in_sem.at[0])
    first.start()
    loads = []
    for e in range(nr):
        t = row_at[(e + 1) % nr]
        cut = pl.ds(t * chunk, chunk)
        load = pltpu.make_async_copy(adj_hbm.at[cut], adj.at[cut], a_sem.at[e])
        load.start()
        loads.append(load)
    small = []
    for n, (src, dst) in enumerate(((weight_hbm, weight_ref), (bias_hbm, bias_ref), (og_hbm, og_ref))):
        load = pltpu.make_async_copy(src, dst, in_sem.at[n + 1])
        load.start()
        small.append(load)

    def blocks_of(col):
        return xg.at[pl.ds(col * own_blocks, own_blocks)]

    xg[nc * own_blocks] = jnp.zeros(xg.shape[1:], xg.dtype)
    first.wait()
    enter(nc, nr)

    copies = []
    for d in range(1, n_out):
        copy = send(blocks_of(c), blocks_of(c), f_send.at[d], f_recv.at[d], {"col": ahead[d]})
        copy.start()
        copies.append(copy)
    pair = []
    copy = send(blocks_of(c), blocks_of(c), p_send.at[0], p_recv.at[0], {"col": partner})
    copy.start()
    pair.append(copy)
    for d in range(1, n_out):
        copies[d - 1].wait_recv()
        came = blocks_of(behind[d])
        copy = send(came, came, p_send.at[d], p_recv.at[d], {"col": partner})
        copy.start()
        pair.append(copy)
    for copy in pair:
        copy.wait_recv()
    for copy in copies + pair:
        copy.wait_send()

    pace = math.gcd(chunk, 2)
    row_copies = []
    for e in range(nr):
        far = (e + 1) % nr
        t = row_at[far]
        loads[e].wait()

        def block_rows(n, carry, t=t, far=far):
            for i in range(pace):
                i = n * pace + i
                b = t * chunk + i
                count = counts_ref[0, b]
                picked = [
                    xg[jnp.where(s < count, cols_ref[s, b], nc * own_blocks)] for s in range(per_row)
                ]
                got = jnp.dot(adj[b], jnp.concatenate(picked, axis=0), preferred_element_type=F32)
                cut = pl.ds(pl.multiple_of(i * tile, tile), tile)
                if far:
                    part[far - 1, cut, :] = got.astype(BF16)
                else:
                    own[cut, :] = got
            return carry

        lax.fori_loop(0, chunk // pace, block_rows, 0)
        if far:
            copy = send(
                part.at[far - 1], rbuf.at[far - 1], r_send.at[far - 1], r_recv.at[far - 1], {"row": t}
            )
            copy.start()
            row_copies.append(copy)
    summed = own[...]
    for copy in row_copies:
        copy.wait_recv()
    for e in range(nr - 1):
        summed = summed + rbuf[e].astype(F32)
    hidden = summed.astype(BF16)
    for load in small:
        load.wait()
    preact = jnp.dot(hidden, weight_ref[...], preferred_element_type=F32) + bias_ref[...]
    sig = jax.nn.sigmoid(preact)
    pre_grad = og_ref[...].astype(F32) * (sig * (1.0 + preact * (1.0 - sig)))
    half = pre_grad.astype(BF16)
    dest = lax.dot_general(
        half, weight_ref[...], (((1,), (1,)), ((), ())), preferred_element_type=F32
    )
    gg[r] = dest.astype(BF16)
    grad_copies = []
    for e in range(1, nr):
        copy = send(gg.at[r], gg.at[r], g_send.at[e - 1], g_recv.at[e - 1], {"row": row_at[e]})
        copy.start()
        grad_copies.append(copy)
    act_ref[...] = (preact * sig).astype(BF16)
    feat = hidden.shape[1]
    cut = feat // nc
    w_out[:, pl.ds(0, cut), :] = scale * lax.dot_general(
        hidden, half, (((0,), (0,)), ((), ())), preferred_element_type=F32
    ).reshape(nc, cut, feat)
    w_out[:, pl.ds(cut, 8), :] = jnp.broadcast_to(
        scale * jnp.sum(pre_grad, axis=0, keepdims=True), (nc, 8, feat)
    )
    w_copies = []
    for d in range(1, nc):
        there = lax.rem(c + d, nc)
        copy = send(w_out.at[there], w_in.at[d - 1], w_send.at[d - 1], w_recv.at[d - 1], {"col": there})
        copy.start()
        w_copies.append(copy)
    total = w_out[c]
    for d in range(1, nc):
        w_copies[d - 1].wait_recv()
        total = total + w_in[d - 1]
    wb_ref[...] = total
    for copy in grad_copies:
        copy.wait_recv()
    grads_ref[...] = gg[...].reshape(grads_ref.shape)
    for copy in row_copies + grad_copies + w_copies:
        copy.wait_send()


def backward_kernel(cols_ref, counts_ref, adj_ref, grad_ref, out_ref, *accs):
    blocks, tile, slot_width = adj_ref.shape
    per_row = slot_width // tile
    dead = out_ref.shape[0]
    for acc in accs:
        acc[...] = jnp.zeros_like(acc)

    def block_row(b, carry):
        contrib = lax.dot_general(
            adj_ref[b], grad_ref[pl.ds(pl.multiple_of(b * tile, tile), tile), :],
            (((0,), (0,)), ((), ())), preferred_element_type=F32,
        )
        count = counts_ref[0, b]
        for s in range(per_row):
            acc = accs[s % len(accs)]
            j = jnp.where(s < count, cols_ref[s, b], dead)
            acc[j] = acc[j] + contrib[s * tile : (s + 1) * tile]
        return carry

    lax.fori_loop(0, blocks, block_row, 0)
    total = accs[0][pl.ds(0, dead)]
    for acc in accs[1:]:
        total = total + acc[pl.ds(0, dead)]
    out_ref[...] = total.astype(BF16)


def scatter_kernel(
    nc, nr, part_ref, wb_ref, out_ref, wg_ref, bg_ref,
    from_pair, send_buf, from_chip, w_row, w_all,
    p_send, p_recv, s_send, s_recv, wr_send, wr_recv, wa_send, wa_recv,
):
    n_out = nc // 2
    c, partner, ahead, behind = col_peers(nc)
    r = lax.axis_index("row")
    row_at = [lax.rem(r + e, nr) for e in range(nr)]
    partner_ahead = [x + partner - c for x in ahead]
    enter(nc, nr)

    started = []

    def go(*args):
        copy = send(*args)
        copy.start()
        started.append(copy)
        return copy

    order = list(range(1, n_out)) + [0]
    pair = {}
    for d in order:
        pair[d] = go(part_ref.at[partner_ahead[d]], from_pair.at[d], p_send.at[d], p_recv.at[d], {"col": partner})
    w_row[r] = wb_ref[...]
    w_copies = [
        go(w_row.at[r], w_row.at[r], wr_send.at[e - 1], wr_recv.at[e - 1], {"row": row_at[e]})
        for e in range(1, nr)
    ]
    copies = []
    for d in order:
        pair[d].wait_recv()
        both = part_ref[ahead[d]].astype(F32) + from_pair[d].astype(F32)
        if d:
            send_buf[d - 1] = both.astype(BF16)
            copies.append(go(
                send_buf.at[d - 1], from_chip.at[d - 1], s_send.at[d - 1], s_recv.at[d - 1], {"col": ahead[d]}
            ))
    for copy in w_copies:
        copy.wait_recv()
    total = w_row[0]
    for n in range(1, nr):
        total = total + w_row[n]
    w_all[c] = total
    w_copies = []
    for d in range(1, nc):
        where = {"col": lax.rem(c + d, nc)}
        w_copies.append(go(w_all.at[c], w_all.at[c], wa_send.at[d - 1], wa_recv.at[d - 1], where))
    for copy in copies:
        copy.wait_recv()
    for d in range(1, n_out):
        both = both + from_chip[d - 1].astype(F32)
    out_ref[...] = both.astype(BF16)
    for copy in w_copies:
        copy.wait_recv()
    cut = wg_ref.shape[0] // nc
    for n in range(nc):
        wg_ref[pl.ds(n * cut, cut), :] = w_all[n, pl.ds(0, cut), :]
    bg_ref[...] = w_all[0, pl.ds(cut, 1), :]
    for copy in started:
        copy.wait_send()


def on_device(mesh, features, adjacency, tile_cols, row_counts, weight, bias, out_grad):
    blocks, tile, slot_width = adjacency.shape
    own_rows, feat = features.shape
    nc, nr = mesh.shape["col"], mesh.shape["row"]
    n_out = nc // 2
    col_blocks = nc * own_rows // tile
    scale = 1.0 / math.sqrt(own_rows * nc * nr)
    cut = feat // nc

    vmem = pl.BlockSpec(memory_space=pltpu.VMEM)
    smem = pl.BlockSpec(memory_space=pltpu.SMEM)
    hbm = pl.BlockSpec(memory_space=pltpu.HBM)
    dma = pltpu.SemaphoreType.DMA
    rows = blocks * tile // nr
    tile_flops = 2 * blocks * tile * slot_width * feat
    activations, grads, wb = pl.pallas_call(
        functools.partial(forward_kernel, nc, nr, scale),
        out_shape=(
            jax.ShapeDtypeStruct((rows, feat), BF16),
            jax.ShapeDtypeStruct((blocks * tile, feat), BF16),
            jax.ShapeDtypeStruct((cut + 8, feat), F32),
        ),
        in_specs=[smem, smem, hbm, hbm, hbm, hbm, hbm],
        out_specs=(vmem, vmem, vmem),
        scratch_shapes=[
            pltpu.VMEM((col_blocks + 1, tile, feat), BF16),
            pltpu.VMEM(adjacency.shape, BF16),
            pltpu.VMEM((feat, feat), BF16),
            pltpu.VMEM((1, feat), F32),
            pltpu.VMEM((rows, feat), BF16),
            pltpu.VMEM((rows, feat), F32),
            pltpu.VMEM((nr - 1, rows, feat), BF16),
            pltpu.VMEM((nr - 1, rows, feat), BF16),
            pltpu.VMEM((nr, rows, feat), BF16),
            pltpu.VMEM((nc, cut + 8, feat), F32),
            pltpu.VMEM((nc - 1, cut + 8, feat), F32),
            dma((4,)), dma((nr,)), dma((n_out,)), dma((n_out,)), dma((n_out,)), dma((n_out,)),
            dma((nr - 1,)), dma((nr - 1,)), dma((nr - 1,)), dma((nr - 1,)), dma((nc - 1,)), dma((nc - 1,)),
        ],
        compiler_params=pltpu.CompilerParams(
            collective_id=0, has_side_effects=True, vmem_limit_bytes=56 * MIB
        ),
        cost_estimate=pl.CostEstimate(
            flops=tile_flops, bytes_accessed=adjacency.size * 2, transcendentals=rows * feat
        ),
    )(
        tile_cols.T, row_counts.T, features.reshape(own_rows // tile, tile, feat), adjacency, weight,
        bias.reshape(1, -1), out_grad,
    )

    partial = pl.pallas_call(
        backward_kernel,
        out_shape=jax.ShapeDtypeStruct((col_blocks, tile, feat), BF16),
        in_specs=[smem, smem, vmem, vmem],
        out_specs=vmem,
        scratch_shapes=[pltpu.VMEM((col_blocks + 1, tile, feat), F32) for unused in range(2)],
        compiler_params=pltpu.CompilerParams(vmem_limit_bytes=32 * MIB),
        cost_estimate=pl.CostEstimate(
            flops=tile_flops * 8, bytes_accessed=adjacency.size * 2, transcendentals=0
        ),
    )(tile_cols.T, row_counts.T, adjacency, grads)

    feature_grad, weight_grad, bias_grad = pl.pallas_call(
        functools.partial(scatter_kernel, nc, nr),
        out_shape=(
            jax.ShapeDtypeStruct((own_rows, feat), BF16),
            jax.ShapeDtypeStruct((feat, feat), F32),
            jax.ShapeDtypeStruct((1, feat), F32),
        ),
        in_specs=[vmem, vmem],
        out_specs=(vmem, vmem, vmem),
        scratch_shapes=[
            pltpu.VMEM((n_out, own_rows, feat), BF16),
            pltpu.VMEM((n_out - 1, own_rows, feat), BF16),
            pltpu.VMEM((n_out - 1, own_rows, feat), BF16),
            pltpu.VMEM((nr, cut + 8, feat), F32),
            pltpu.VMEM((nc, cut + 8, feat), F32),
            dma((n_out,)), dma((n_out,)), dma((n_out - 1,)), dma((n_out - 1,)),
            dma((nr - 1,)), dma((nr - 1,)), dma((nc - 1,)), dma((nc - 1,)),
        ],
        compiler_params=pltpu.CompilerParams(
            collective_id=1, has_side_effects=True, vmem_limit_bytes=20 * MIB
        ),
        cost_estimate=pl.CostEstimate(
            flops=own_rows * nc * feat, bytes_accessed=8 * own_rows * nc * feat, transcendentals=0
        ),
    )(partial.reshape(nc, own_rows, feat), wb)
    return (activations, feature_grad, weight_grad, bias_grad.reshape(-1))


def solution(mesh):
    placed = (
        P(("groups", "row", "col"), None),
        P(("groups", "col"), None, "row"),
        P(("groups", "col"), "row"),
        P(("groups", "col"), "row"),
        P(),
        P(),
        P(("groups", "col", "row"), None),
    )
    return jax.shard_map(
        functools.partial(on_device, mesh),
        mesh=mesh,
        in_specs=placed,
        out_specs=(
            P(("groups", "col", "row"), None),
            P(("groups", "row", "col"), None),
            P("groups", None),
            P("groups"),
        ),
        check_vma=False,
    )
```

```python
import functools
import math

import jax
import jax.numpy as jnp
from jax import lax
from jax.experimental import pallas as pl
from jax.experimental.pallas import tpu as pltpu
from jax.sharding import PartitionSpec as P

MESH = pl.DeviceIdType.MESH
F32, BF16 = jnp.float32, jnp.bfloat16
MIB = 1024 * 1024


def col_peers(nc):
    c = lax.axis_index("col")
    outer, core, n_out = c // 2, c % 2, nc // 2
    partner = outer * 2 + (1 - core)
    ahead = [lax.rem(outer + d, n_out) * 2 + core for d in range(n_out)]
    behind = [lax.rem(outer - d + n_out, n_out) * 2 + core for d in range(n_out)]
    return c, partner, ahead, behind


def send(src, dst, send_sem, recv_sem, where):
    return pltpu.make_async_remote_copy(
        src_ref=src, dst_ref=dst, send_sem=send_sem, recv_sem=recv_sem,
        device_id=where, device_id_type=MESH,
    )


def enter(nc, nr):
    c, r = lax.axis_index("col"), lax.axis_index("row")
    barrier = pltpu.get_barrier_semaphore()
    for d in range(1, nc):
        pl.semaphore_signal(barrier, inc=1, device_id={"col": lax.rem(c + d, nc)}, device_id_type=MESH)
    for e in range(1, nr):
        pl.semaphore_signal(barrier, inc=1, device_id={"row": lax.rem(r + e, nr)}, device_id_type=MESH)
    pl.semaphore_wait(barrier, nc - 1 + nr - 1)


def forward_kernel(
    nc, nr, scale, cols_ref, counts_ref, feat_hbm, adj_hbm, weight_hbm, bias_hbm, og_hbm,
    act_ref, grads_ref, wb_ref,
    xg, adj, weight_ref, bias_ref, og_ref, own, part, rbuf, gg, w_out, w_in, w_all,
    in_sem, a_sem, f_send, f_recv, p_send, p_recv, r_send, r_recv, g_send, g_recv, w_send, w_recv, wa_send, wa_recv,
):
    blocks, tile, slot_width = adj.shape
    per_row = slot_width // tile
    chunk = blocks // nr
    rows = chunk * tile
    n_out = nc // 2
    own_blocks = feat_hbm.shape[0]
    c, partner, ahead, behind = col_peers(nc)
    r = lax.axis_index("row")
    row_at = [lax.rem(r + e, nr) for e in range(nr)]

    mine = xg.at[pl.ds(c * own_blocks, own_blocks)]
    first = pltpu.make_async_copy(feat_hbm, mine, in_sem.at[0])
    first.start()
    loads = []
    for e in range(nr):
        t = row_at[(e + 1) % nr]
        cut = pl.ds(t * chunk, chunk)
        load = pltpu.make_async_copy(adj_hbm.at[cut], adj.at[cut], a_sem.at[e])
        load.start()
        loads.append(load)
    small = []
    for n, (src, dst) in enumerate(((weight_hbm, weight_ref), (bias_hbm, bias_ref), (og_hbm, og_ref))):
        load = pltpu.make_async_copy(src, dst, in_sem.at[n + 1])
        load.start()
        small.append(load)

    def blocks_of(col):
        return xg.at[pl.ds(col * own_blocks, own_blocks)]

    xg[nc * own_blocks] = jnp.zeros(xg.shape[1:], xg.dtype)
    first.wait()
    enter(nc, nr)

    copies = []
    for d in range(1, n_out):
        copy = send(blocks_of(c), blocks_of(c), f_send.at[d], f_recv.at[d], {"col": ahead[d]})
        copy.start()
        copies.append(copy)
    pair = []
    copy = send(blocks_of(c), blocks_of(c), p_send.at[0], p_recv.at[0], {"col": partner})
    copy.start()
    pair.append(copy)
    for d in range(1, n_out):
        copies[d - 1].wait_recv()
        came = blocks_of(behind[d])
        copy = send(came, came, p_send.at[d], p_recv.at[d], {"col": partner})
        copy.start()
        pair.append(copy)
    for copy in pair:
        copy.wait_recv()
    for copy in copies + pair:
        copy.wait_send()

    pace = math.gcd(chunk, 2)
    row_copies = []
    for e in range(nr):
        far = (e + 1) % nr
        t = row_at[far]
        loads[e].wait()

        def block_rows(n, carry, t=t, far=far):
            for i in range(pace):
                i = n * pace + i
                b = t * chunk + i
                count = counts_ref[0, b]
                picked = [
                    xg[jnp.where(s < count, cols_ref[s, b], nc * own_blocks)] for s in range(per_row)
                ]
                got = jnp.dot(adj[b], jnp.concatenate(picked, axis=0), preferred_element_type=F32)
                cut = pl.ds(pl.multiple_of(i * tile, tile), tile)
                if far:
                    part[far - 1, cut, :] = got.astype(BF16)
                else:
                    own[cut, :] = got
            return carry

        lax.fori_loop(0, chunk // pace, block_rows, 0)
        if far:
            copy = send(
                part.at[far - 1], rbuf.at[far - 1], r_send.at[far - 1], r_recv.at[far - 1], {"row": t}
            )
            copy.start()
            row_copies.append(copy)
    summed = own[...]
    for copy in row_copies:
        copy.wait_recv()
    for e in range(nr - 1):
        summed = summed + rbuf[e].astype(F32)
    hidden = summed.astype(BF16)
    for load in small:
        load.wait()
    preact = jnp.dot(hidden, weight_ref[...], preferred_element_type=F32) + bias_ref[...]
    sig = jax.nn.sigmoid(preact)
    pre_grad = og_ref[...].astype(F32) * (sig * (1.0 + preact * (1.0 - sig)))
    half = pre_grad.astype(BF16)
    dest = lax.dot_general(
        half, weight_ref[...], (((1,), (1,)), ((), ())), preferred_element_type=F32
    )
    gg[r] = dest.astype(BF16)

    def hop(t, step):
        way = 0 if step > 0 else 1
        return send(gg.at[t], gg.at[t], g_send.at[way, t], g_recv.at[t], {"row": r + step})

    for step in (1, -1):
        @pl.when((r + step >= 0) & (r + step < nr))
        def start_chain(step=step):
            hop(r, step).start()
    act_ref[...] = (preact * sig).astype(BF16)
    feat = hidden.shape[1]
    cut = feat // nc
    w_out[:, pl.ds(0, cut), :] = scale * lax.dot_general(
        hidden, half, (((0,), (0,)), ((), ())), preferred_element_type=F32
    ).reshape(nc, cut, feat)
    w_out[:, pl.ds(cut, 8), :] = jnp.broadcast_to(
        scale * jnp.sum(pre_grad, axis=0, keepdims=True), (nc, 8, feat)
    )
    w_copies = []
    for d in range(1, nc):
        there = lax.rem(c + d, nc)
        copy = send(w_out.at[there], w_in.at[d - 1], w_send.at[d - 1], w_recv.at[d - 1], {"col": there})
        copy.start()
        w_copies.append(copy)
    for k in range(1, nr):
        if k == min(2, nr - 1):
            total = w_out[c]
            for d in range(1, nc):
                w_copies[d - 1].wait_recv()
                total = total + w_in[d - 1]
            w_all[c] = total
            for d in range(1, nc):
                there = lax.rem(c + d, nc)
                copy = send(w_all.at[c], w_all.at[c], wa_send.at[d - 1], wa_recv.at[d - 1], {"col": there})
                copy.start()
                w_copies.append(copy)
        for step in (1, -1):
            t = r - k * step
            came = (t >= 0) & (t < nr)

            @pl.when(came)
            def arrive(t=t, step=step):
                hop(t, step).wait_recv()

            @pl.when(came & (r + step >= 0) & (r + step < nr))
            def pass_on(t=t, step=step):
                hop(t, step).start()
    for k in range(nr):
        for step in (1, -1):
            t = r - k * step

            @pl.when((t >= 0) & (t < nr) & (r + step >= 0) & (r + step < nr))
            def sent(t=t, step=step):
                hop(t, step).wait_send()
    for copy in w_copies[nc - 1 :]:
        copy.wait_recv()
    for n in range(nc):
        wb_ref[pl.ds(n * cut, cut), :] = w_all[n, pl.ds(0, cut), :]
    wb_ref[pl.ds(feat, 8), :] = w_all[0, pl.ds(cut, 8), :]
    grads_ref[...] = gg[...].reshape(grads_ref.shape)
    for copy in row_copies + w_copies:
        copy.wait_send()


def backward_kernel(cols_ref, counts_ref, adj_ref, grad_ref, out_ref, *accs):
    blocks, tile, slot_width = adj_ref.shape
    per_row = slot_width // tile
    dead = out_ref.shape[0]
    for acc in accs:
        acc[...] = jnp.zeros_like(acc)

    pace = math.gcd(blocks, 2)

    def block_rows(n, carry):
        contribs = []
        for i in range(pace):
            b = n * pace + i
            contribs.append(lax.dot_general(
                adj_ref[b], grad_ref[pl.ds(pl.multiple_of(b * tile, tile), tile), :],
                (((0,), (0,)), ((), ())), preferred_element_type=F32,
            ))
        for s in range(per_row):
            for i in range(pace):
                b = n * pace + i
                acc = accs[2 * i + s % 2]
                j = jnp.where(s < counts_ref[0, b], cols_ref[s, b], dead)
                acc[j] = acc[j] + contribs[i][s * tile : (s + 1) * tile]
        return carry

    lax.fori_loop(0, blocks // pace, block_rows, 0)
    total = accs[0][pl.ds(0, dead)]
    for acc in accs[1:]:
        total = total + acc[pl.ds(0, dead)]
    out_ref[...] = total.astype(BF16)


def scatter_kernel(
    nc, nr, part_ref, wb_ref, out_ref, wg_ref, bg_ref,
    from_pair, send_buf, from_chip, w_row,
    p_send, p_recv, s_send, s_recv, wr_send, wr_recv,
):
    n_out = nc // 2
    c, partner, ahead, behind = col_peers(nc)
    r = lax.axis_index("row")
    row_at = [lax.rem(r + e, nr) for e in range(nr)]
    partner_ahead = [x + partner - c for x in ahead]
    enter(nc, nr)

    started = []

    def go(*args):
        copy = send(*args)
        copy.start()
        started.append(copy)
        return copy

    order = list(range(1, n_out)) + [0]
    pair = {}
    for d in order:
        pair[d] = go(part_ref.at[partner_ahead[d]], from_pair.at[d], p_send.at[d], p_recv.at[d], {"col": partner})
    w_row[r] = wb_ref[...]
    w_copies = [
        go(w_row.at[r], w_row.at[r], wr_send.at[e - 1], wr_recv.at[e - 1], {"row": row_at[e]})
        for e in range(1, nr)
    ]
    copies = []
    for d in order:
        pair[d].wait_recv()
        both = part_ref[ahead[d]].astype(F32) + from_pair[d].astype(F32)
        if d:
            send_buf[d - 1] = both.astype(BF16)
            copies.append(go(
                send_buf.at[d - 1], from_chip.at[d - 1], s_send.at[d - 1], s_recv.at[d - 1], {"col": ahead[d]}
            ))
    for copy in copies:
        copy.wait_recv()
    for d in range(1, n_out):
        both = both + from_chip[d - 1].astype(F32)
    out_ref[...] = both.astype(BF16)
    for copy in w_copies:
        copy.wait_recv()
    total = w_row[0]
    for n in range(1, nr):
        total = total + w_row[n]
    feat = wg_ref.shape[0]
    wg_ref[...] = total[:feat]
    bg_ref[...] = total[feat : feat + 1]
    for copy in started:
        copy.wait_send()


def on_device(mesh, features, adjacency, tile_cols, row_counts, weight, bias, out_grad):
    blocks, tile, slot_width = adjacency.shape
    own_rows, feat = features.shape
    nc, nr = mesh.shape["col"], mesh.shape["row"]
    n_out = nc // 2
    col_blocks = nc * own_rows // tile
    scale = 1.0 / math.sqrt(own_rows * nc * nr)
    cut = feat // nc

    vmem = pl.BlockSpec(memory_space=pltpu.VMEM)
    smem = pl.BlockSpec(memory_space=pltpu.SMEM)
    hbm = pl.BlockSpec(memory_space=pltpu.HBM)
    dma = pltpu.SemaphoreType.DMA
    rows = blocks * tile // nr
    tile_flops = 2 * blocks * tile * slot_width * feat
    activations, grads, wb = pl.pallas_call(
        functools.partial(forward_kernel, nc, nr, scale),
        out_shape=(
            jax.ShapeDtypeStruct((rows, feat), BF16),
            jax.ShapeDtypeStruct((blocks * tile, feat), BF16),
            jax.ShapeDtypeStruct((feat + 8, feat), F32),
        ),
        in_specs=[smem, smem, hbm, hbm, hbm, hbm, hbm],
        out_specs=(vmem, vmem, vmem),
        scratch_shapes=[
            pltpu.VMEM((col_blocks + 1, tile, feat), BF16),
            pltpu.VMEM(adjacency.shape, BF16),
            pltpu.VMEM((feat, feat), BF16),
            pltpu.VMEM((1, feat), F32),
            pltpu.VMEM((rows, feat), BF16),
            pltpu.VMEM((rows, feat), F32),
            pltpu.VMEM((nr - 1, rows, feat), BF16),
            pltpu.VMEM((nr - 1, rows, feat), BF16),
            pltpu.VMEM((nr, rows, feat), BF16),
            pltpu.VMEM((nc, cut + 8, feat), F32),
            pltpu.VMEM((nc - 1, cut + 8, feat), F32),
            pltpu.VMEM((nc, cut + 8, feat), F32),
            dma((4,)), dma((nr,)), dma((n_out,)), dma((n_out,)), dma((n_out,)), dma((n_out,)),
            dma((nr - 1,)), dma((nr - 1,)), dma((2, nr)), dma((nr,)),
            dma((nc - 1,)), dma((nc - 1,)), dma((nc - 1,)), dma((nc - 1,)),
        ],
        compiler_params=pltpu.CompilerParams(
            collective_id=0, has_side_effects=True, vmem_limit_bytes=56 * MIB
        ),
        cost_estimate=pl.CostEstimate(
            flops=tile_flops, bytes_accessed=adjacency.size * 2, transcendentals=rows * feat
        ),
    )(
        tile_cols.T, row_counts.T, features.reshape(own_rows // tile, tile, feat), adjacency, weight,
        bias.reshape(1, -1), out_grad,
    )

    partial = pl.pallas_call(
        backward_kernel,
        out_shape=jax.ShapeDtypeStruct((col_blocks, tile, feat), BF16),
        in_specs=[smem, smem, vmem, vmem],
        out_specs=vmem,
        scratch_shapes=[pltpu.VMEM((col_blocks + 1, tile, feat), F32) for unused in range(4)],
        compiler_params=pltpu.CompilerParams(vmem_limit_bytes=32 * MIB),
        cost_estimate=pl.CostEstimate(
            flops=tile_flops * 8, bytes_accessed=adjacency.size * 2, transcendentals=0
        ),
    )(tile_cols.T, row_counts.T, adjacency, grads)

    feature_grad, weight_grad, bias_grad = pl.pallas_call(
        functools.partial(scatter_kernel, nc, nr),
        out_shape=(
            jax.ShapeDtypeStruct((own_rows, feat), BF16),
            jax.ShapeDtypeStruct((feat, feat), F32),
            jax.ShapeDtypeStruct((1, feat), F32),
        ),
        in_specs=[vmem, vmem],
        out_specs=(vmem, vmem, vmem),
        scratch_shapes=[
            pltpu.VMEM((n_out, own_rows, feat), BF16),
            pltpu.VMEM((n_out - 1, own_rows, feat), BF16),
            pltpu.VMEM((n_out - 1, own_rows, feat), BF16),
            pltpu.VMEM((nr, feat + 8, feat), F32),
            dma((n_out,)), dma((n_out,)), dma((n_out - 1,)), dma((n_out - 1,)),
            dma((nr - 1,)), dma((nr - 1,)),
        ],
        compiler_params=pltpu.CompilerParams(
            collective_id=1, has_side_effects=True, vmem_limit_bytes=20 * MIB
        ),
        cost_estimate=pl.CostEstimate(
            flops=own_rows * nc * feat, bytes_accessed=8 * own_rows * nc * feat, transcendentals=0
        ),
    )(partial.reshape(nc, own_rows, feat), wb)
    return (activations, feature_grad, weight_grad, bias_grad.reshape(-1))


def solution(mesh):
    placed = (
        P(("groups", "row", "col"), None),
        P(("groups", "col"), None, "row"),
        P(("groups", "col"), "row"),
        P(("groups", "col"), "row"),
        P(),
        P(),
        P(("groups", "col", "row"), None),
    )
    return jax.shard_map(
        functools.partial(on_device, mesh),
        mesh=mesh,
        in_specs=placed,
        out_specs=(
            P(("groups", "col", "row"), None),
            P(("groups", "row", "col"), None),
            P("groups", None),
            P("groups"),
        ),
        check_vma=False,
    )
```

```python
import functools
import math

import jax
import jax.numpy as jnp
from jax import lax
from jax.experimental import pallas as pl
from jax.experimental.pallas import tpu as pltpu
from jax.sharding import PartitionSpec as P

MESH = pl.DeviceIdType.MESH
F32, BF16 = jnp.float32, jnp.bfloat16
MIB = 1024 * 1024


def col_peers(nc):
    c = lax.axis_index("col")
    outer, core, n_out = c // 2, c % 2, nc // 2
    partner = outer * 2 + (1 - core)
    ahead = [lax.rem(outer + d, n_out) * 2 + core for d in range(n_out)]
    behind = [lax.rem(outer - d + n_out, n_out) * 2 + core for d in range(n_out)]
    return c, partner, ahead, behind


def send(src, dst, send_sem, recv_sem, where):
    return pltpu.make_async_remote_copy(
        src_ref=src, dst_ref=dst, send_sem=send_sem, recv_sem=recv_sem,
        device_id=where, device_id_type=MESH,
    )


def enter(nc, nr):
    c, r = lax.axis_index("col"), lax.axis_index("row")
    barrier = pltpu.get_barrier_semaphore()
    for d in range(1, nc):
        pl.semaphore_signal(barrier, inc=1, device_id={"col": lax.rem(c + d, nc)}, device_id_type=MESH)
    for e in range(1, nr):
        pl.semaphore_signal(barrier, inc=1, device_id={"row": lax.rem(r + e, nr)}, device_id_type=MESH)
    pl.semaphore_wait(barrier, nc - 1 + nr - 1)


def forward_kernel(
    nc, nr, scale, cols_ref, counts_ref, feat_hbm, adj_hbm, weight_hbm, bias_hbm, og_hbm,
    act_ref, grads_ref, wb_ref,
    xg, adj, weight_ref, bias_ref, og_ref, own, part, rbuf, gg, w_out, w_in, w_all,
    in_sem, a_sem, f_send, f_recv, p_send, p_recv, r_send, r_recv, g_send, g_recv, w_send, w_recv, wa_send, wa_recv,
):
    blocks, tile, slot_width = adj.shape
    per_row = slot_width // tile
    chunk = blocks // nr
    rows = chunk * tile
    n_out = nc // 2
    own_blocks = feat_hbm.shape[0]
    c, partner, ahead, behind = col_peers(nc)
    r = lax.axis_index("row")
    row_at = [lax.rem(r + e, nr) for e in range(nr)]

    mine = xg.at[pl.ds(c * own_blocks, own_blocks)]
    first = pltpu.make_async_copy(feat_hbm, mine, in_sem.at[0])
    first.start()
    loads = []
    for e in range(nr):
        t = row_at[(e + 1) % nr]
        cut = pl.ds(t * chunk, chunk)
        load = pltpu.make_async_copy(adj_hbm.at[cut], adj.at[cut], a_sem.at[e])
        load.start()
        loads.append(load)
    small = []
    for n, (src, dst) in enumerate(((weight_hbm, weight_ref), (bias_hbm, bias_ref), (og_hbm, og_ref))):
        load = pltpu.make_async_copy(src, dst, in_sem.at[n + 1])
        load.start()
        small.append(load)

    def blocks_of(col):
        return xg.at[pl.ds(col * own_blocks, own_blocks)]

    xg[nc * own_blocks] = jnp.zeros(xg.shape[1:], xg.dtype)
    first.wait()
    enter(nc, nr)

    copies = []
    for d in range(1, n_out):
        copy = send(blocks_of(c), blocks_of(c), f_send.at[d], f_recv.at[d], {"col": ahead[d]})
        copy.start()
        copies.append(copy)
    pair = []
    copy = send(blocks_of(c), blocks_of(c), p_send.at[0], p_recv.at[0], {"col": partner})
    copy.start()
    pair.append(copy)
    for d in range(1, n_out):
        copies[d - 1].wait_recv()
        came = blocks_of(behind[d])
        copy = send(came, came, p_send.at[d], p_recv.at[d], {"col": partner})
        copy.start()
        pair.append(copy)
    for copy in pair:
        copy.wait_recv()
    for copy in copies + pair:
        copy.wait_send()

    pace = math.gcd(chunk, 4)
    row_copies = []
    for e in range(nr):
        far = (e + 1) % nr
        t = row_at[far]
        loads[e].wait()

        def block_rows(n, carry, t=t, far=far):
            for i in range(pace):
                i = n * pace + i
                b = t * chunk + i
                count = counts_ref[0, b]
                picked = [
                    xg[jnp.where(s < count, cols_ref[s, b], nc * own_blocks)] for s in range(per_row)
                ]
                got = jnp.dot(adj[b], jnp.concatenate(picked, axis=0), preferred_element_type=F32)
                cut = pl.ds(pl.multiple_of(i * tile, tile), tile)
                if far:
                    part[far - 1, cut, :] = got.astype(BF16)
                else:
                    own[cut, :] = got
            return carry

        lax.fori_loop(0, chunk // pace, block_rows, 0)
        if far:
            copy = send(
                part.at[far - 1], rbuf.at[far - 1], r_send.at[far - 1], r_recv.at[far - 1], {"row": t}
            )
            copy.start()
            row_copies.append(copy)
    summed = own[...]
    for copy in row_copies:
        copy.wait_recv()
    for e in range(nr - 1):
        summed = summed + rbuf[e].astype(F32)
    hidden = summed.astype(BF16)
    for load in small:
        load.wait()
    preact = jnp.dot(hidden, weight_ref[...], preferred_element_type=F32) + bias_ref[...]
    sig = jax.nn.sigmoid(preact)
    pre_grad = og_ref[...].astype(F32) * (sig * (1.0 + preact * (1.0 - sig)))
    half = pre_grad.astype(BF16)
    dest = lax.dot_general(
        half, weight_ref[...], (((1,), (1,)), ((), ())), preferred_element_type=F32
    )
    gg[r] = dest.astype(BF16)

    def hop(t, step):
        way = 0 if step > 0 else 1
        return send(gg.at[t], gg.at[t], g_send.at[way, t], g_recv.at[t], {"row": r + step})

    for step in (1, -1):
        @pl.when((r + step >= 0) & (r + step < nr))
        def start_chain(step=step):
            hop(r, step).start()
    act_ref[...] = (preact * sig).astype(BF16)
    feat = hidden.shape[1]
    cut = feat // nc
    w_out[:, pl.ds(0, cut), :] = scale * lax.dot_general(
        hidden, half, (((0,), (0,)), ((), ())), preferred_element_type=F32
    ).reshape(nc, cut, feat)
    w_out[:, pl.ds(cut, 8), :] = jnp.broadcast_to(
        scale * jnp.sum(pre_grad, axis=0, keepdims=True), (nc, 8, feat)
    )
    w_copies = []
    for d in range(1, nc):
        there = lax.rem(c + d, nc)
        copy = send(w_out.at[there], w_in.at[d - 1], w_send.at[d - 1], w_recv.at[d - 1], {"col": there})
        copy.start()
        w_copies.append(copy)
    for k in range(1, nr):
        if k == min(2, nr - 1):
            total = w_out[c]
            for d in range(1, nc):
                w_copies[d - 1].wait_recv()
                total = total + w_in[d - 1]
            w_all[c] = total
            for d in range(1, nc):
                there = lax.rem(c + d, nc)
                copy = send(w_all.at[c], w_all.at[c], wa_send.at[d - 1], wa_recv.at[d - 1], {"col": there})
                copy.start()
                w_copies.append(copy)
        for step in (1, -1):
            t = r - k * step
            came = (t >= 0) & (t < nr)

            @pl.when(came)
            def arrive(t=t, step=step):
                hop(t, step).wait_recv()

            @pl.when(came & (r + step >= 0) & (r + step < nr))
            def pass_on(t=t, step=step):
                hop(t, step).start()
    for k in range(nr):
        for step in (1, -1):
            t = r - k * step

            @pl.when((t >= 0) & (t < nr) & (r + step >= 0) & (r + step < nr))
            def sent(t=t, step=step):
                hop(t, step).wait_send()
    for copy in w_copies[nc - 1 :]:
        copy.wait_recv()
    for n in range(nc):
        wb_ref[pl.ds(n * cut, cut), :] = w_all[n, pl.ds(0, cut), :]
    wb_ref[pl.ds(feat, 8), :] = w_all[0, pl.ds(cut, 8), :]
    grads_ref[...] = gg[...].reshape(grads_ref.shape)
    for copy in row_copies + w_copies:
        copy.wait_send()


def backward_kernel(cols_ref, counts_ref, adj_ref, grad_ref, act_hbm, out_ref, act_out, sem, *accs):
    blocks, tile, slot_width = adj_ref.shape
    per_row = slot_width // tile
    dead = out_ref.shape[0]
    hand_out = pltpu.make_async_copy(act_hbm, act_out, sem)
    hand_out.start()
    for acc in accs:
        acc[...] = jnp.zeros_like(acc)

    pace = math.gcd(blocks, 4)

    def block_rows(n, carry):
        contribs = []
        for i in range(pace):
            b = n * pace + i
            contribs.append(lax.dot_general(
                adj_ref[b], grad_ref[pl.ds(pl.multiple_of(b * tile, tile), tile), :],
                (((0,), (0,)), ((), ())), preferred_element_type=F32,
            ))
        for s in range(per_row):
            for i in range(pace):
                b = n * pace + i
                acc = accs[i]
                j = jnp.where(s < counts_ref[0, b], cols_ref[s, b], dead)
                acc[j] = acc[j] + contribs[i][s * tile : (s + 1) * tile]
        return carry

    lax.fori_loop(0, blocks // pace, block_rows, 0)
    total = accs[0][pl.ds(0, dead)]
    for acc in accs[1:]:
        total = total + acc[pl.ds(0, dead)]
    out_ref[...] = total.astype(BF16)
    hand_out.wait()


def scatter_kernel(
    nc, nr, part_ref, wb_ref, out_ref, wg_ref, bg_ref,
    from_pair, send_buf, from_chip, w_row,
    p_send, p_recv, s_send, s_recv, wr_send, wr_recv,
):
    n_out = nc // 2
    c, partner, ahead, behind = col_peers(nc)
    r = lax.axis_index("row")
    row_at = [lax.rem(r + e, nr) for e in range(nr)]
    partner_ahead = [x + partner - c for x in ahead]
    enter(nc, nr)

    started = []

    def go(*args):
        copy = send(*args)
        copy.start()
        started.append(copy)
        return copy

    order = list(range(1, n_out)) + [0]
    pair = {}
    for d in order:
        pair[d] = go(part_ref.at[partner_ahead[d]], from_pair.at[d], p_send.at[d], p_recv.at[d], {"col": partner})
    w_row[r] = wb_ref[...]
    w_copies = [
        go(w_row.at[r], w_row.at[r], wr_send.at[e - 1], wr_recv.at[e - 1], {"row": row_at[e]})
        for e in range(1, nr)
    ]
    copies = []
    for d in order:
        pair[d].wait_recv()
        both = part_ref[ahead[d]].astype(F32) + from_pair[d].astype(F32)
        if d:
            send_buf[d - 1] = both.astype(BF16)
            copies.append(go(
                send_buf.at[d - 1], from_chip.at[d - 1], s_send.at[d - 1], s_recv.at[d - 1], {"col": ahead[d]}
            ))
    for copy in copies:
        copy.wait_recv()
    for d in range(1, n_out):
        both = both + from_chip[d - 1].astype(F32)
    out_ref[...] = both.astype(BF16)
    for copy in w_copies:
        copy.wait_recv()
    total = w_row[0]
    for n in range(1, nr):
        total = total + w_row[n]
    feat = wg_ref.shape[0]
    wg_ref[...] = total[:feat]
    bg_ref[...] = total[feat : feat + 1]
    for copy in started:
        copy.wait_send()


def on_device(mesh, features, adjacency, tile_cols, row_counts, weight, bias, out_grad):
    blocks, tile, slot_width = adjacency.shape
    own_rows, feat = features.shape
    nc, nr = mesh.shape["col"], mesh.shape["row"]
    n_out = nc // 2
    col_blocks = nc * own_rows // tile
    scale = 1.0 / math.sqrt(own_rows * nc * nr)
    cut = feat // nc

    vmem = pl.BlockSpec(memory_space=pltpu.VMEM)
    smem = pl.BlockSpec(memory_space=pltpu.SMEM)
    hbm = pl.BlockSpec(memory_space=pltpu.HBM)
    dma = pltpu.SemaphoreType.DMA
    rows = blocks * tile // nr
    tile_flops = 2 * blocks * tile * slot_width * feat
    activations, grads, wb = pl.pallas_call(
        functools.partial(forward_kernel, nc, nr, scale),
        out_shape=(
            jax.ShapeDtypeStruct((rows, feat), BF16),
            jax.ShapeDtypeStruct((blocks * tile, feat), BF16),
            jax.ShapeDtypeStruct((feat + 8, feat), F32),
        ),
        in_specs=[smem, smem, hbm, hbm, hbm, hbm, hbm],
        out_specs=(vmem, vmem, vmem),
        scratch_shapes=[
            pltpu.VMEM((col_blocks + 1, tile, feat), BF16),
            pltpu.VMEM(adjacency.shape, BF16),
            pltpu.VMEM((feat, feat), BF16),
            pltpu.VMEM((1, feat), F32),
            pltpu.VMEM((rows, feat), BF16),
            pltpu.VMEM((rows, feat), F32),
            pltpu.VMEM((nr - 1, rows, feat), BF16),
            pltpu.VMEM((nr - 1, rows, feat), BF16),
            pltpu.VMEM((nr, rows, feat), BF16),
            pltpu.VMEM((nc, cut + 8, feat), F32),
            pltpu.VMEM((nc - 1, cut + 8, feat), F32),
            pltpu.VMEM((nc, cut + 8, feat), F32),
            dma((4,)), dma((nr,)), dma((n_out,)), dma((n_out,)), dma((n_out,)), dma((n_out,)),
            dma((nr - 1,)), dma((nr - 1,)), dma((2, nr)), dma((nr,)),
            dma((nc - 1,)), dma((nc - 1,)), dma((nc - 1,)), dma((nc - 1,)),
        ],
        compiler_params=pltpu.CompilerParams(
            collective_id=0, has_side_effects=True, vmem_limit_bytes=56 * MIB
        ),
        cost_estimate=pl.CostEstimate(
            flops=tile_flops, bytes_accessed=adjacency.size * 2, transcendentals=rows * feat
        ),
    )(
        tile_cols.T, row_counts.T, features.reshape(own_rows // tile, tile, feat), adjacency, weight,
        bias.reshape(1, -1), out_grad,
    )

    partial, activations = pl.pallas_call(
        backward_kernel,
        out_shape=(
            jax.ShapeDtypeStruct((col_blocks, tile, feat), BF16),
            jax.ShapeDtypeStruct((rows, feat), BF16),
        ),
        in_specs=[smem, smem, vmem, vmem, hbm],
        out_specs=(vmem, hbm),
        scratch_shapes=[dma] + [pltpu.VMEM((col_blocks + 1, tile, feat), F32) for unused in range(4)],
        compiler_params=pltpu.CompilerParams(vmem_limit_bytes=32 * MIB),
        cost_estimate=pl.CostEstimate(
            flops=tile_flops * 8, bytes_accessed=adjacency.size * 2, transcendentals=0
        ),
    )(tile_cols.T, row_counts.T, adjacency, grads, activations)

    feature_grad, weight_grad, bias_grad = pl.pallas_call(
        functools.partial(scatter_kernel, nc, nr),
        out_shape=(
            jax.ShapeDtypeStruct((own_rows, feat), BF16),
            jax.ShapeDtypeStruct((feat, feat), F32),
            jax.ShapeDtypeStruct((1, feat), F32),
        ),
        in_specs=[vmem, vmem],
        out_specs=(vmem, vmem, vmem),
        scratch_shapes=[
            pltpu.VMEM((n_out, own_rows, feat), BF16),
            pltpu.VMEM((n_out - 1, own_rows, feat), BF16),
            pltpu.VMEM((n_out - 1, own_rows, feat), BF16),
            pltpu.VMEM((nr, feat + 8, feat), F32),
            dma((n_out,)), dma((n_out,)), dma((n_out - 1,)), dma((n_out - 1,)),
            dma((nr - 1,)), dma((nr - 1,)),
        ],
        compiler_params=pltpu.CompilerParams(
            collective_id=1, has_side_effects=True, vmem_limit_bytes=20 * MIB
        ),
        cost_estimate=pl.CostEstimate(
            flops=own_rows * nc * feat, bytes_accessed=8 * own_rows * nc * feat, transcendentals=0
        ),
    )(partial.reshape(nc, own_rows, feat), wb)
    return (activations, feature_grad, weight_grad, bias_grad.reshape(-1))


def solution(mesh):
    placed = (
        P(("groups", "row", "col"), None),
        P(("groups", "col"), None, "row"),
        P(("groups", "col"), "row"),
        P(("groups", "col"), "row"),
        P(),
        P(),
        P(("groups", "col", "row"), None),
    )
    return jax.shard_map(
        functools.partial(on_device, mesh),
        mesh=mesh,
        in_specs=placed,
        out_specs=(
            P(("groups", "col", "row"), None),
            P(("groups", "row", "col"), None),
            P("groups", None),
            P("groups"),
        ),
        check_vma=False,
    )
```

```python
import functools
import math

import jax
import jax.numpy as jnp
from jax import lax
from jax.experimental import pallas as pl
from jax.experimental.pallas import tpu as pltpu
from jax.sharding import PartitionSpec as P

MESH = pl.DeviceIdType.MESH
F32, BF16 = jnp.float32, jnp.bfloat16
MIB = 1024 * 1024


def col_peers(nc):
    c = lax.axis_index("col")
    outer, core, n_out = c // 2, c % 2, nc // 2
    partner = outer * 2 + (1 - core)
    ahead = [lax.rem(outer + d, n_out) * 2 + core for d in range(n_out)]
    behind = [lax.rem(outer - d + n_out, n_out) * 2 + core for d in range(n_out)]
    return c, partner, ahead, behind


def send(src, dst, send_sem, recv_sem, where):
    return pltpu.make_async_remote_copy(
        src_ref=src, dst_ref=dst, send_sem=send_sem, recv_sem=recv_sem,
        device_id=where, device_id_type=MESH,
    )


def enter(nc, nr):
    c, r = lax.axis_index("col"), lax.axis_index("row")
    barrier = pltpu.get_barrier_semaphore()
    for d in range(1, nc):
        pl.semaphore_signal(barrier, inc=1, device_id={"col": lax.rem(c + d, nc)}, device_id_type=MESH)
    for e in range(1, nr):
        pl.semaphore_signal(barrier, inc=1, device_id={"row": lax.rem(r + e, nr)}, device_id_type=MESH)
    pl.semaphore_wait(barrier, nc - 1 + nr - 1)


def forward_kernel(
    nc, nr, scale, cols_ref, counts_ref, feat_hbm, adj_hbm, weight_hbm, bias_hbm, og_hbm,
    grads_ref, wb_ref,
    xg, adj, weight_ref, bias_ref, og_ref, own, part, rbuf, gg, w_out, w_in, w_all,
    in_sem, a_sem, f_send, f_recv, p_send, p_recv, r_send, r_recv, g_send, g_recv, w_send, w_recv, wa_send, wa_recv,
):
    blocks, tile, slot_width = adj.shape
    per_row = slot_width // tile
    chunk = blocks // nr
    rows = chunk * tile
    n_out = nc // 2
    own_blocks = feat_hbm.shape[0]
    c, partner, ahead, behind = col_peers(nc)
    r = lax.axis_index("row")
    row_at = [lax.rem(r + e, nr) for e in range(nr)]

    mine = xg.at[pl.ds(c * own_blocks, own_blocks)]
    first = pltpu.make_async_copy(feat_hbm, mine, in_sem.at[0])
    first.start()
    loads = []
    for e in range(nr):
        t = row_at[(e + 1) % nr]
        cut = pl.ds(t * chunk, chunk)
        load = pltpu.make_async_copy(adj_hbm.at[cut], adj.at[cut], a_sem.at[e])
        load.start()
        loads.append(load)
    small = []
    for n, (src, dst) in enumerate(((weight_hbm, weight_ref), (bias_hbm, bias_ref), (og_hbm, og_ref))):
        load = pltpu.make_async_copy(src, dst, in_sem.at[n + 1])
        load.start()
        small.append(load)

    def blocks_of(col):
        return xg.at[pl.ds(col * own_blocks, own_blocks)]

    xg[nc * own_blocks] = jnp.zeros(xg.shape[1:], xg.dtype)
    first.wait()
    enter(nc, nr)

    copies = []
    for d in range(1, n_out):
        copy = send(blocks_of(c), blocks_of(c), f_send.at[d], f_recv.at[d], {"col": ahead[d]})
        copy.start()
        copies.append(copy)
    pair = []
    copy = send(blocks_of(c), blocks_of(c), p_send.at[0], p_recv.at[0], {"col": partner})
    copy.start()
    pair.append(copy)
    for d in range(1, n_out):
        copies[d - 1].wait_recv()
        came = blocks_of(behind[d])
        copy = send(came, came, p_send.at[d], p_recv.at[d], {"col": partner})
        copy.start()
        pair.append(copy)
    for copy in pair:
        copy.wait_recv()
    for copy in copies + pair:
        copy.wait_send()

    pace = math.gcd(chunk, 4)
    row_copies = []
    for e in range(nr):
        far = (e + 1) % nr
        t = row_at[far]
        loads[e].wait()

        def block_rows(n, carry, t=t, far=far):
            for i in range(pace):
                i = n * pace + i
                b = t * chunk + i
                count = counts_ref[0, b]
                picked = [
                    xg[jnp.where(s < count, cols_ref[s, b], nc * own_blocks)] for s in range(per_row)
                ]
                got = jnp.dot(adj[b], jnp.concatenate(picked, axis=0), preferred_element_type=F32)
                cut = pl.ds(pl.multiple_of(i * tile, tile), tile)
                if far:
                    part[far - 1, cut, :] = got.astype(BF16)
                else:
                    own[cut, :] = got
            return carry

        lax.fori_loop(0, chunk // pace, block_rows, 0)
        if far:
            copy = send(
                part.at[far - 1], rbuf.at[far - 1], r_send.at[far - 1], r_recv.at[far - 1], {"row": t}
            )
            copy.start()
            row_copies.append(copy)
    summed = own[...]
    for copy in row_copies:
        copy.wait_recv()
    for e in range(nr - 1):
        summed = summed + rbuf[e].astype(F32)
    hidden = summed.astype(BF16)
    for load in small:
        load.wait()
    preact = jnp.dot(hidden, weight_ref[...], preferred_element_type=F32) + bias_ref[...]
    sig = jax.nn.sigmoid(preact)
    pre_grad = og_ref[...].astype(F32) * (sig * (1.0 + preact * (1.0 - sig)))
    half = pre_grad.astype(BF16)
    dest = lax.dot_general(
        half, weight_ref[...], (((1,), (1,)), ((), ())), preferred_element_type=F32
    )
    gg[r] = dest.astype(BF16)

    def hop(t, step):
        way = 0 if step > 0 else 1
        return send(gg.at[t], gg.at[t], g_send.at[way, t], g_recv.at[t], {"row": r + step})

    for step in (1, -1):
        @pl.when((r + step >= 0) & (r + step < nr))
        def start_chain(step=step):
            hop(r, step).start()
    grads_ref[pl.ds(nr * rows, rows), :] = (preact * sig).astype(BF16)
    feat = hidden.shape[1]
    cut = feat // nc
    w_out[:, pl.ds(0, cut), :] = scale * lax.dot_general(
        hidden, half, (((0,), (0,)), ((), ())), preferred_element_type=F32
    ).reshape(nc, cut, feat)
    w_out[:, pl.ds(cut, 8), :] = jnp.broadcast_to(
        scale * jnp.sum(pre_grad, axis=0, keepdims=True), (nc, 8, feat)
    )
    w_copies = []
    for d in range(1, nc):
        there = lax.rem(c + d, nc)
        copy = send(w_out.at[there], w_in.at[d - 1], w_send.at[d - 1], w_recv.at[d - 1], {"col": there})
        copy.start()
        w_copies.append(copy)
    for k in range(1, nr):
        if k == min(2, nr - 1):
            total = w_out[c]
            for d in range(1, nc):
                w_copies[d - 1].wait_recv()
                total = total + w_in[d - 1]
            w_all[c] = total
            for d in range(1, nc):
                there = lax.rem(c + d, nc)
                copy = send(w_all.at[c], w_all.at[c], wa_send.at[d - 1], wa_recv.at[d - 1], {"col": there})
                copy.start()
                w_copies.append(copy)
        for step in (1, -1):
            t = r - k * step
            came = (t >= 0) & (t < nr)

            @pl.when(came)
            def arrive(t=t, step=step):
                hop(t, step).wait_recv()

            @pl.when(came & (r + step >= 0) & (r + step < nr))
            def pass_on(t=t, step=step):
                hop(t, step).start()
    for k in range(nr):
        for step in (1, -1):
            t = r - k * step

            @pl.when((t >= 0) & (t < nr) & (r + step >= 0) & (r + step < nr))
            def sent(t=t, step=step):
                hop(t, step).wait_send()
    for copy in w_copies[nc - 1 :]:
        copy.wait_recv()
    for n in range(nc):
        wb_ref[pl.ds(n * cut, cut), :] = w_all[n, pl.ds(0, cut), :]
    wb_ref[pl.ds(feat, 8), :] = w_all[0, pl.ds(cut, 8), :]
    grads_ref[pl.ds(0, nr * rows), :] = gg[...].reshape(nr * rows, feat)
    for copy in row_copies + w_copies:
        copy.wait_send()


def backward_kernel(cols_ref, counts_ref, adj_ref, grad_ref, out_ref, act_out, sem, *accs):
    blocks, tile, slot_width = adj_ref.shape
    per_row = slot_width // tile
    dead = out_ref.shape[0]
    hand_out = pltpu.make_async_copy(grad_ref.at[pl.ds(blocks * tile, act_out.shape[0])], act_out, sem)
    hand_out.start()
    for acc in accs:
        acc[...] = jnp.zeros_like(acc)

    pace = math.gcd(blocks, 8)

    def block_rows(n, carry):
        contribs = []
        for i in range(pace):
            b = n * pace + i
            contribs.append(lax.dot_general(
                adj_ref[b], grad_ref[pl.ds(pl.multiple_of(b * tile, tile), tile), :],
                (((0,), (0,)), ((), ())), preferred_element_type=F32,
            ))
        for s in range(per_row):
            for i in range(pace):
                b = n * pace + i
                acc = accs[i % 4]
                j = jnp.where(s < counts_ref[0, b], cols_ref[s, b], dead)
                acc[j] = acc[j] + contribs[i][s * tile : (s + 1) * tile]
        return carry

    lax.fori_loop(0, blocks // pace, block_rows, 0)
    total = accs[0][pl.ds(0, dead)]
    for acc in accs[1:]:
        total = total + acc[pl.ds(0, dead)]
    out_ref[...] = total.astype(BF16)
    hand_out.wait()


def scatter_kernel(
    nc, nr, part_ref, wb_ref, out_ref, wg_ref, bg_ref,
    from_pair, send_buf, from_chip, w_row,
    p_send, p_recv, s_send, s_recv, wr_send, wr_recv,
):
    n_out = nc // 2
    c, partner, ahead, behind = col_peers(nc)
    r = lax.axis_index("row")
    row_at = [lax.rem(r + e, nr) for e in range(nr)]
    partner_ahead = [x + partner - c for x in ahead]
    enter(nc, nr)

    started = []

    def go(*args):
        copy = send(*args)
        copy.start()
        started.append(copy)
        return copy

    order = list(range(1, n_out)) + [0]
    pair = {}
    for d in order:
        pair[d] = go(part_ref.at[partner_ahead[d]], from_pair.at[d], p_send.at[d], p_recv.at[d], {"col": partner})
    w_row[r] = wb_ref[...]
    w_copies = [
        go(w_row.at[r], w_row.at[r], wr_send.at[e - 1], wr_recv.at[e - 1], {"row": row_at[e]})
        for e in range(1, nr)
    ]
    copies = []
    for d in order:
        pair[d].wait_recv()
        both = part_ref[ahead[d]].astype(F32) + from_pair[d].astype(F32)
        if d:
            send_buf[d - 1] = both.astype(BF16)
            copies.append(go(
                send_buf.at[d - 1], from_chip.at[d - 1], s_send.at[d - 1], s_recv.at[d - 1], {"col": ahead[d]}
            ))
    for copy in copies:
        copy.wait_recv()
    for d in range(1, n_out):
        both = both + from_chip[d - 1].astype(F32)
    out_ref[...] = both.astype(BF16)
    for copy in w_copies:
        copy.wait_recv()
    total = w_row[0]
    for n in range(1, nr):
        total = total + w_row[n]
    feat = wg_ref.shape[0]
    wg_ref[...] = total[:feat]
    bg_ref[...] = total[feat : feat + 1]
    for copy in started:
        copy.wait_send()


def on_device(mesh, features, adjacency, tile_cols, row_counts, weight, bias, out_grad):
    blocks, tile, slot_width = adjacency.shape
    own_rows, feat = features.shape
    nc, nr = mesh.shape["col"], mesh.shape["row"]
    n_out = nc // 2
    col_blocks = nc * own_rows // tile
    scale = 1.0 / math.sqrt(own_rows * nc * nr)
    cut = feat // nc

    vmem = pl.BlockSpec(memory_space=pltpu.VMEM)
    smem = pl.BlockSpec(memory_space=pltpu.SMEM)
    hbm = pl.BlockSpec(memory_space=pltpu.HBM)
    dma = pltpu.SemaphoreType.DMA
    rows = blocks * tile // nr
    tile_flops = 2 * blocks * tile * slot_width * feat
    grads, wb = pl.pallas_call(
        functools.partial(forward_kernel, nc, nr, scale),
        out_shape=(
            jax.ShapeDtypeStruct((blocks * tile + rows, feat), BF16),
            jax.ShapeDtypeStruct((feat + 8, feat), F32),
        ),
        in_specs=[smem, smem, hbm, hbm, hbm, hbm, hbm],
        out_specs=(vmem, vmem),
        scratch_shapes=[
            pltpu.VMEM((col_blocks + 1, tile, feat), BF16),
            pltpu.VMEM(adjacency.shape, BF16),
            pltpu.VMEM((feat, feat), BF16),
            pltpu.VMEM((1, feat), F32),
            pltpu.VMEM((rows, feat), BF16),
            pltpu.VMEM((rows, feat), F32),
            pltpu.VMEM((nr - 1, rows, feat), BF16),
            pltpu.VMEM((nr - 1, rows, feat), BF16),
            pltpu.VMEM((nr, rows, feat), BF16),
            pltpu.VMEM((nc, cut + 8, feat), F32),
            pltpu.VMEM((nc - 1, cut + 8, feat), F32),
            pltpu.VMEM((nc, cut + 8, feat), F32),
            dma((4,)), dma((nr,)), dma((n_out,)), dma((n_out,)), dma((n_out,)), dma((n_out,)),
            dma((nr - 1,)), dma((nr - 1,)), dma((2, nr)), dma((nr,)),
            dma((nc - 1,)), dma((nc - 1,)), dma((nc - 1,)), dma((nc - 1,)),
        ],
        compiler_params=pltpu.CompilerParams(
            collective_id=0, has_side_effects=True, vmem_limit_bytes=56 * MIB
        ),
        cost_estimate=pl.CostEstimate(
            flops=tile_flops, bytes_accessed=adjacency.size * 2, transcendentals=rows * feat
        ),
    )(
        tile_cols.T, row_counts.T, features.reshape(own_rows // tile, tile, feat), adjacency, weight,
        bias.reshape(1, -1), out_grad,
    )

    partial, activations = pl.pallas_call(
        backward_kernel,
        out_shape=(
            jax.ShapeDtypeStruct((col_blocks, tile, feat), BF16),
            jax.ShapeDtypeStruct((rows, feat), BF16),
        ),
        in_specs=[smem, smem, vmem, vmem],
        out_specs=(vmem, hbm),
        scratch_shapes=[dma] + [pltpu.VMEM((col_blocks + 1, tile, feat), F32) for unused in range(4)],
        compiler_params=pltpu.CompilerParams(vmem_limit_bytes=32 * MIB),
        cost_estimate=pl.CostEstimate(
            flops=tile_flops * 8, bytes_accessed=adjacency.size * 2, transcendentals=0
        ),
    )(tile_cols.T, row_counts.T, adjacency, grads)

    feature_grad, weight_grad, bias_grad = pl.pallas_call(
        functools.partial(scatter_kernel, nc, nr),
        out_shape=(
            jax.ShapeDtypeStruct((own_rows, feat), BF16),
            jax.ShapeDtypeStruct((feat, feat), F32),
            jax.ShapeDtypeStruct((1, feat), F32),
        ),
        in_specs=[vmem, vmem],
        out_specs=(vmem, vmem, vmem),
        scratch_shapes=[
            pltpu.VMEM((n_out, own_rows, feat), BF16),
            pltpu.VMEM((n_out - 1, own_rows, feat), BF16),
            pltpu.VMEM((n_out - 1, own_rows, feat), BF16),
            pltpu.VMEM((nr, feat + 8, feat), F32),
            dma((n_out,)), dma((n_out,)), dma((n_out - 1,)), dma((n_out - 1,)),
            dma((nr - 1,)), dma((nr - 1,)),
        ],
        compiler_params=pltpu.CompilerParams(
            collective_id=1, has_side_effects=True, vmem_limit_bytes=20 * MIB
        ),
        cost_estimate=pl.CostEstimate(
            flops=own_rows * nc * feat, bytes_accessed=8 * own_rows * nc * feat, transcendentals=0
        ),
    )(partial.reshape(nc, own_rows, feat), wb)
    return (activations, feature_grad, weight_grad, bias_grad.reshape(-1))


def solution(mesh):
    placed = (
        P(("groups", "row", "col"), None),
        P(("groups", "col"), None, "row"),
        P(("groups", "col"), "row"),
        P(("groups", "col"), "row"),
        P(),
        P(),
        P(("groups", "col", "row"), None),
    )
    return jax.shard_map(
        functools.partial(on_device, mesh),
        mesh=mesh,
        in_specs=placed,
        out_specs=(
            P(("groups", "col", "row"), None),
            P(("groups", "row", "col"), None),
            P("groups", None),
            P("groups"),
        ),
        check_vma=False,
    )
```

```python
import functools
import math

import jax
import jax.numpy as jnp
from jax import lax
from jax.experimental import pallas as pl
from jax.experimental.pallas import tpu as pltpu
from jax.sharding import PartitionSpec as P

MESH = pl.DeviceIdType.MESH
F32, BF16 = jnp.float32, jnp.bfloat16
MIB = 1024 * 1024


def col_peers(nc):
    c = lax.axis_index("col")
    outer, core, n_out = c // 2, c % 2, nc // 2
    partner = outer * 2 + (1 - core)
    ahead = [lax.rem(outer + d, n_out) * 2 + core for d in range(n_out)]
    behind = [lax.rem(outer - d + n_out, n_out) * 2 + core for d in range(n_out)]
    return c, partner, ahead, behind


def send(src, dst, send_sem, recv_sem, where):
    return pltpu.make_async_remote_copy(
        src_ref=src, dst_ref=dst, send_sem=send_sem, recv_sem=recv_sem,
        device_id=where, device_id_type=MESH,
    )


def enter(nc, nr):
    c, r = lax.axis_index("col"), lax.axis_index("row")
    barrier = pltpu.get_barrier_semaphore()
    for d in range(1, nc):
        pl.semaphore_signal(barrier, inc=1, device_id={"col": lax.rem(c + d, nc)}, device_id_type=MESH)
    for e in range(1, nr):
        pl.semaphore_signal(barrier, inc=1, device_id={"row": lax.rem(r + e, nr)}, device_id_type=MESH)
    pl.semaphore_wait(barrier, nc - 1 + nr - 1)


def forward_kernel(
    nc, nr, scale, cols_ref, counts_ref, feat_hbm, adj_hbm, weight_hbm, bias_hbm, og_hbm,
    grads_ref, wb_ref,
    xg, adj, weight_ref, bias_ref, og_ref, own, part, rbuf, gg, w_out, w_in, w_all,
    in_sem, a_sem, f_send, f_recv, p_send, p_recv, r_send, r_recv, g_send, g_recv, w_send, w_recv, wa_send, wa_recv,
):
    blocks, tile, slot_width = adj.shape
    per_row = slot_width // tile
    chunk = blocks // nr
    rows = chunk * tile
    n_out = nc // 2
    own_blocks = feat_hbm.shape[0]
    c, partner, ahead, behind = col_peers(nc)
    r = lax.axis_index("row")
    row_at = [lax.rem(r + e, nr) for e in range(nr)]

    mine = xg.at[pl.ds(c * own_blocks, own_blocks)]
    first = pltpu.make_async_copy(feat_hbm, mine, in_sem.at[0])
    first.start()
    loads = []
    for e in range(nr):
        t = row_at[(e + 1) % nr]
        cut = pl.ds(t * chunk, chunk)
        load = pltpu.make_async_copy(adj_hbm.at[cut], adj.at[cut], a_sem.at[e])
        load.start()
        loads.append(load)
    small = []
    for n, (src, dst) in enumerate(((weight_hbm, weight_ref), (bias_hbm, bias_ref), (og_hbm, og_ref))):
        load = pltpu.make_async_copy(src, dst, in_sem.at[n + 1])
        load.start()
        small.append(load)

    def blocks_of(col):
        return xg.at[pl.ds(col * own_blocks, own_blocks)]

    xg[nc * own_blocks] = jnp.zeros(xg.shape[1:], xg.dtype)
    first.wait()
    enter(nc, nr)

    copies = []
    for d in range(1, n_out):
        copy = send(blocks_of(c), blocks_of(c), f_send.at[d], f_recv.at[d], {"col": ahead[d]})
        copy.start()
        copies.append(copy)
    pair = []
    copy = send(blocks_of(c), blocks_of(c), p_send.at[0], p_recv.at[0], {"col": partner})
    copy.start()
    pair.append(copy)
    for d in range(1, n_out):
        copies[d - 1].wait_recv()
        came = blocks_of(behind[d])
        copy = send(came, came, p_send.at[d], p_recv.at[d], {"col": partner})
        copy.start()
        pair.append(copy)
    for copy in pair:
        copy.wait_recv()
    for copy in copies + pair:
        copy.wait_send()

    pace = math.gcd(chunk, 4)
    row_copies = []
    for e in range(nr):
        far = (e + 1) % nr
        t = row_at[far]
        loads[e].wait()

        def block_rows(n, carry, t=t, far=far):
            for i in range(pace):
                i = n * pace + i
                b = t * chunk + i
                count = counts_ref[0, b]
                picked = [
                    xg[jnp.where(s < count, cols_ref[s, b], nc * own_blocks)] for s in range(per_row)
                ]
                got = jnp.dot(adj[b], jnp.concatenate(picked, axis=0), preferred_element_type=F32)
                cut = pl.ds(pl.multiple_of(i * tile, tile), tile)
                if far:
                    part[far - 1, cut, :] = got.astype(BF16)
                else:
                    own[cut, :] = got
            return carry

        lax.fori_loop(0, chunk // pace, block_rows, 0)
        if far:
            copy = send(
                part.at[far - 1], rbuf.at[far - 1], r_send.at[far - 1], r_recv.at[far - 1], {"row": t}
            )
            copy.start()
            row_copies.append(copy)
    summed = own[...]
    for copy in row_copies:
        copy.wait_recv()
    for e in range(nr - 1):
        summed = summed + rbuf[e].astype(F32)
    hidden = summed.astype(BF16)
    for load in small:
        load.wait()
    preact = jnp.dot(hidden, weight_ref[...], preferred_element_type=F32) + bias_ref[...]
    sig = jax.nn.sigmoid(preact)
    pre_grad = og_ref[...].astype(F32) * (sig * (1.0 + preact * (1.0 - sig)))
    half = pre_grad.astype(BF16)
    dest = lax.dot_general(
        half, weight_ref[...], (((1,), (1,)), ((), ())), preferred_element_type=F32
    )
    gg[r] = dest.astype(BF16)

    def hop(t, step):
        way = 0 if step > 0 else 1
        return send(gg.at[t], gg.at[t], g_send.at[way, t], g_recv.at[t], {"row": r + step})

    for step in (1, -1):
        @pl.when((r + step >= 0) & (r + step < nr))
        def start_chain(step=step):
            hop(r, step).start()
    grads_ref[pl.ds(nr * rows, rows), :] = (preact * sig).astype(BF16)
    feat = hidden.shape[1]
    cut = feat // nc
    w_out[:, pl.ds(0, cut), :] = scale * lax.dot_general(
        hidden, half, (((0,), (0,)), ((), ())), preferred_element_type=F32
    ).reshape(nc, cut, feat)
    w_out[:, pl.ds(cut, 8), :] = jnp.broadcast_to(
        scale * jnp.sum(pre_grad, axis=0, keepdims=True), (nc, 8, feat)
    )
    w_copies = []
    for d in range(1, nc):
        there = lax.rem(c + d, nc)
        copy = send(w_out.at[there], w_in.at[d - 1], w_send.at[d - 1], w_recv.at[d - 1], {"col": there})
        copy.start()
        w_copies.append(copy)
    for k in range(1, nr):
        if k == min(2, nr - 1):
            total = w_out[c]
            for d in range(1, nc):
                w_copies[d - 1].wait_recv()
                total = total + w_in[d - 1]
            w_all[c] = total
            for d in range(1, nc):
                there = lax.rem(c + d, nc)
                copy = send(w_all.at[c], w_all.at[c], wa_send.at[d - 1], wa_recv.at[d - 1], {"col": there})
                copy.start()
                w_copies.append(copy)
        for step in (1, -1):
            t = r - k * step
            came = (t >= 0) & (t < nr)

            @pl.when(came)
            def arrive(t=t, step=step):
                hop(t, step).wait_recv()

            @pl.when(came & (r + step >= 0) & (r + step < nr))
            def pass_on(t=t, step=step):
                hop(t, step).start()
    for k in range(nr):
        for step in (1, -1):
            t = r - k * step

            @pl.when((t >= 0) & (t < nr) & (r + step >= 0) & (r + step < nr))
            def sent(t=t, step=step):
                hop(t, step).wait_send()
    for copy in w_copies[nc - 1 :]:
        copy.wait_recv()
    for n in range(nc):
        wb_ref[pl.ds(n * cut, cut), :] = w_all[n, pl.ds(0, cut), :]
    wb_ref[pl.ds(feat, 8), :] = w_all[0, pl.ds(cut, 8), :]
    grads_ref[pl.ds(0, nr * rows), :] = gg[...].reshape(nr * rows, feat)
    for copy in row_copies + w_copies:
        copy.wait_send()


def backward_kernel(cols_ref, counts_ref, adj_ref, grad_ref, out_ref, act_out, sem, *accs):
    blocks, tile, slot_width = adj_ref.shape
    per_row = slot_width // tile
    dead = out_ref.shape[0]
    hand_out = pltpu.make_async_copy(grad_ref.at[pl.ds(blocks * tile, act_out.shape[0])], act_out, sem)
    hand_out.start()
    for acc in accs:
        acc[...] = jnp.zeros_like(acc)

    pace = math.gcd(blocks, 4)

    def block_rows(n, carry):
        contribs = []
        for i in range(pace):
            b = n * pace + i
            contribs.append(lax.dot_general(
                adj_ref[b], grad_ref[pl.ds(pl.multiple_of(b * tile, tile), tile), :],
                (((0,), (0,)), ((), ())), preferred_element_type=F32,
            ))
        for s in range(per_row):
            for i in range(pace):
                b = n * pace + i
                acc = accs[i]
                j = jnp.where(s < counts_ref[0, b], cols_ref[s, b], dead)
                acc[j] = acc[j] + contribs[i][s * tile : (s + 1) * tile]
        return carry

    lax.fori_loop(0, blocks // pace, block_rows, 0)
    total = accs[0][pl.ds(0, dead)]
    for acc in accs[1:]:
        total = total + acc[pl.ds(0, dead)]
    out_ref[...] = total.astype(BF16)
    hand_out.wait()


def scatter_kernel(
    nc, nr, part_ref, wb_ref, out_ref, wg_ref, bg_ref,
    from_pair, send_buf, from_chip, w_row,
    p_send, p_recv, s_send, s_recv, wr_send, wr_recv,
):
    n_out = nc // 2
    c, partner, ahead, behind = col_peers(nc)
    r = lax.axis_index("row")
    row_at = [lax.rem(r + e, nr) for e in range(nr)]
    partner_ahead = [x + partner - c for x in ahead]
    enter(nc, nr)

    started = []

    def go(*args):
        copy = send(*args)
        copy.start()
        started.append(copy)
        return copy

    order = list(range(1, n_out)) + [0]
    pair = {}
    for d in order:
        pair[d] = go(part_ref.at[partner_ahead[d]], from_pair.at[d], p_send.at[d], p_recv.at[d], {"col": partner})
    w_row[r] = wb_ref[...]
    w_copies = [
        go(w_row.at[r], w_row.at[r], wr_send.at[e - 1], wr_recv.at[e - 1], {"row": row_at[e]})
        for e in range(1, nr)
    ]
    copies = []
    for d in order:
        pair[d].wait_recv()
        both = part_ref[ahead[d]].astype(F32) + from_pair[d].astype(F32)
        if d:
            send_buf[d - 1] = both.astype(BF16)
            copies.append(go(
                send_buf.at[d - 1], from_chip.at[d - 1], s_send.at[d - 1], s_recv.at[d - 1], {"col": ahead[d]}
            ))
    for copy in copies:
        copy.wait_recv()
    for d in range(1, n_out):
        both = both + from_chip[d - 1].astype(F32)
    out_ref[...] = both.astype(BF16)
    for copy in w_copies:
        copy.wait_recv()
    total = w_row[0]
    for n in range(1, nr):
        total = total + w_row[n]
    feat = wg_ref.shape[0]
    wg_ref[...] = total[:feat]
    bg_ref[...] = total[feat : feat + 1]
    for copy in started:
        copy.wait_send()


def on_device(mesh, features, adjacency, tile_cols, row_counts, weight, bias, out_grad):
    blocks, tile, slot_width = adjacency.shape
    own_rows, feat = features.shape
    nc, nr = mesh.shape["col"], mesh.shape["row"]
    n_out = nc // 2
    col_blocks = nc * own_rows // tile
    scale = 1.0 / math.sqrt(own_rows * nc * nr)
    cut = feat // nc

    vmem = pl.BlockSpec(memory_space=pltpu.VMEM)
    smem = pl.BlockSpec(memory_space=pltpu.SMEM)
    hbm = pl.BlockSpec(memory_space=pltpu.HBM)
    dma = pltpu.SemaphoreType.DMA
    rows = blocks * tile // nr
    tile_flops = 2 * blocks * tile * slot_width * feat
    grads, wb = pl.pallas_call(
        functools.partial(forward_kernel, nc, nr, scale),
        out_shape=(
            jax.ShapeDtypeStruct((blocks * tile + rows, feat), BF16),
            jax.ShapeDtypeStruct((feat + 8, feat), F32),
        ),
        in_specs=[smem, smem, hbm, hbm, hbm, hbm, hbm],
        out_specs=(vmem, vmem),
        scratch_shapes=[
            pltpu.VMEM((col_blocks + 1, tile, feat), BF16),
            pltpu.VMEM(adjacency.shape, BF16),
            pltpu.VMEM((feat, feat), BF16),
            pltpu.VMEM((1, feat), F32),
            pltpu.VMEM((rows, feat), BF16),
            pltpu.VMEM((rows, feat), F32),
            pltpu.VMEM((nr - 1, rows, feat), BF16),
            pltpu.VMEM((nr - 1, rows, feat), BF16),
            pltpu.VMEM((nr, rows, feat), BF16),
            pltpu.VMEM((nc, cut + 8, feat), F32),
            pltpu.VMEM((nc - 1, cut + 8, feat), F32),
            pltpu.VMEM((nc, cut + 8, feat), F32),
            dma((4,)), dma((nr,)), dma((n_out,)), dma((n_out,)), dma((n_out,)), dma((n_out,)),
            dma((nr - 1,)), dma((nr - 1,)), dma((2, nr)), dma((nr,)),
            dma((nc - 1,)), dma((nc - 1,)), dma((nc - 1,)), dma((nc - 1,)),
        ],
        compiler_params=pltpu.CompilerParams(
            collective_id=0, has_side_effects=True, vmem_limit_bytes=56 * MIB
        ),
        cost_estimate=pl.CostEstimate(
            flops=tile_flops, bytes_accessed=adjacency.size * 2, transcendentals=rows * feat
        ),
    )(
        tile_cols.T, row_counts.T, features.reshape(own_rows // tile, tile, feat), adjacency, weight,
        bias.reshape(1, -1), out_grad,
    )

    partial, activations = pl.pallas_call(
        backward_kernel,
        out_shape=(
            jax.ShapeDtypeStruct((col_blocks, tile, feat), BF16),
            jax.ShapeDtypeStruct((rows, feat), BF16),
        ),
        in_specs=[smem, smem, vmem, vmem],
        out_specs=(vmem, hbm),
        scratch_shapes=[dma] + [pltpu.VMEM((col_blocks + 1, tile, feat), F32) for unused in range(4)],
        compiler_params=pltpu.CompilerParams(vmem_limit_bytes=32 * MIB),
        cost_estimate=pl.CostEstimate(
            flops=tile_flops * 8, bytes_accessed=adjacency.size * 2, transcendentals=0
        ),
    )(tile_cols.T, row_counts.T, adjacency, grads)

    feature_grad, weight_grad, bias_grad = pl.pallas_call(
        functools.partial(scatter_kernel, nc, nr),
        out_shape=(
            jax.ShapeDtypeStruct((own_rows, feat), BF16),
            jax.ShapeDtypeStruct((feat, feat), F32),
            jax.ShapeDtypeStruct((1, feat), F32),
        ),
        in_specs=[vmem, vmem],
        out_specs=(vmem, vmem, vmem),
        scratch_shapes=[
            pltpu.VMEM((n_out, own_rows, feat), BF16),
            pltpu.VMEM((n_out - 1, own_rows, feat), BF16),
            pltpu.VMEM((n_out - 1, own_rows, feat), BF16),
            pltpu.VMEM((nr, feat + 8, feat), F32),
            dma((n_out,)), dma((n_out,)), dma((n_out - 1,)), dma((n_out - 1,)),
            dma((nr - 1,)), dma((nr - 1,)),
        ],
        compiler_params=pltpu.CompilerParams(
            collective_id=1, has_side_effects=True, vmem_limit_bytes=20 * MIB
        ),
        cost_estimate=pl.CostEstimate(
            flops=own_rows * nc * feat, bytes_accessed=8 * own_rows * nc * feat, transcendentals=0
        ),
    )(partial.reshape(nc, own_rows, feat), wb)
    return (activations, feature_grad, weight_grad, bias_grad.reshape(-1))


def solution(mesh):
    placed = (
        P(("groups", "row", "col"), None),
        P(("groups", "col"), None, "row"),
        P(("groups", "col"), "row"),
        P(("groups", "col"), "row"),
        P(),
        P(),
        P(("groups", "col", "row"), None),
    )
    return jax.shard_map(
        functools.partial(on_device, mesh),
        mesh=mesh,
        in_specs=placed,
        out_specs=(
            P(("groups", "col", "row"), None),
            P(("groups", "row", "col"), None),
            P("groups", None),
            P("groups"),
        ),
        check_vma=False,
    )
```
